32 devices in a mesh: diag: 8 (over z, x), slab: 4 (over y, core).
Axes of the slice: x: 2, y: 2, z: 4, core: 2. Of those that a mesh axis runs over, the one named last changes fastest.
Arguments:
- left: float32 [8, 768, 768], P('diag', 'slab'), may hold values from -0.355756237 to 0.355756237
- right: float32 [8, 768, 768], P('diag', 'slab'), may hold values from -0.355756237 to 0.355756237
- window_a: float32 [8, 768, 768], P('diag', 'slab'), may hold values from -6 to 6
- window_b: float32 [8, 768, 768], P('diag', 'slab'), may hold values from -6 to 6
- row_slab_a: float32 [8, 512, 768], P('diag', 'slab'), may hold values from -6 to 6
- row_slab_b: float32 [8, 512, 768], P('diag', 'slab'), may hold values from -6 to 6
- column_slab_a: float32 [8, 512, 768], P('diag', 'slab'), may hold values from -6 to 6
- column_slab_b: float32 [8, 512, 768], P('diag', 'slab'), may hold values from -6 to 6
- row_live: int32 [8], P('diag'), may hold values from 256 to 512, as said below
- column_live: int32 [8], P('diag'), may hold values from 256 to 512, as said below
Outputs:
- updated_window_a: float32 [8, 768, 768], P('diag', 'slab')
- updated_window_b: float32 [8, 768, 768], P('diag', 'slab')
- updated_row_slab_a: float32 [8, 512, 768], P('diag', 'slab')
- updated_row_slab_b: float32 [8, 512, 768], P('diag', 'slab')
- updated_column_slab_a: float32 [8, 512, 768], P('diag', 'slab')
- updated_column_slab_b: float32 [8, 512, 768], P('diag', 'slab')
The draws below stay inside these ranges and needn't reach their ends.
Inputs may be any that keep to these rules, and one draw needn't show every extreme that they name: `row_live`: in every draw one window has all 512 positions live and another exactly half of them. `column_live`: in every draw one window has all 512 positions live and another exactly half of them.
All inputs are finite; a program needn't handle non-finite values.
Results may differ from the reference program's by a relative error of at most 0.0002.
Values sent between devices are 32-bit elements; how exact they have to be, the bound alone decides.
A program may use at most 64 MiB of HBM per device.

```python
import math
import jax
import jax.numpy as jnp
from jax import lax

W = 768
OVL = 256
OWNERS = 8
SLAB_LEN = 512


def factor_draw(key):
    full_shape = (OWNERS, W, W)
    entries = jnp.clip(jax.random.normal(key, full_shape, jnp.float32), -6.0, 6.0)
    row_index = lax.broadcasted_iota(jnp.int32, full_shape, 1)
    column_index = lax.broadcasted_iota(jnp.int32, full_shape, 2)
    inside = (row_index < OVL) & (column_index >= W - OVL)
    corner_gain = jnp.where(inside, math.sqrt(0.9 * W / OVL), 1.0)
    return entries * corner_gain / math.sqrt(W)


def draw_left(key, part):
    return factor_draw(jax.random.fold_in(key, 11))


def draw_right(key, part):
    return factor_draw(jax.random.fold_in(key, 23))


def live_draw(key):
    counts = jax.random.randint(key, (OWNERS,), SLAB_LEN // 2, SLAB_LEN + 1, jnp.int32)
    shuffled = jax.random.permutation(jax.random.fold_in(key, 7), OWNERS)
    counts = counts.at[shuffled[0]].set(SLAB_LEN)
    return counts.at[shuffled[1]].set(SLAB_LEN // 2)


def draw_row_live(key, part):
    return live_draw(jax.random.fold_in(key, 31))


def draw_column_live(key, part):
    return live_draw(jax.random.fold_in(key, 37))


def steps_of(rng, extent, pieces, least, top_value):
    gain = 1.0
    for position, blocks in pieces:
        heights = jax.random.uniform(jax.random.fold_in(jax.random.fold_in(rng, 6), position), (blocks,), jnp.float32, least / len(pieces), top_value / len(pieces))
        gain = gain * jnp.repeat(jnp.exp(heights), extent[position] // blocks).reshape((-1,) + (1,) * (len(extent) - 1 - position))
    return gain


def normal_values(own_key, shape, scale, most, pieces=(), dtype=jnp.bfloat16):
    values = jax.random.normal(own_key, shape, jnp.float32) * scale
    if len(pieces) > 0:
        values = steps_of(own_key, shape, pieces, -0.22, 0.18) * values
    return jnp.clip(values, min=-most, max=most).astype(dtype)


def setup_inputs(seed: int = 0) -> dict:
    arg_keys = jax.random.split(jax.random.key(seed), 11)
    left = draw_left(jax.random.fold_in(arg_keys[10], 71), 0)
    right = draw_right(jax.random.fold_in(arg_keys[10], 71), 0)
    window_a = normal_values(arg_keys[2], (OWNERS, W, W), 1.0, 6.0, ((0, 8), (1, 4)), jnp.float32)
    window_b = normal_values(arg_keys[3], (OWNERS, W, W), 1.0, 6.0, ((0, 8), (1, 4)), jnp.float32)
    row_slab_a = normal_values(arg_keys[4], (OWNERS, SLAB_LEN, W), 1.0, 6.0, ((0, 8), (1, 4)), jnp.float32)
    row_slab_b = normal_values(arg_keys[5], (OWNERS, SLAB_LEN, W), 1.0, 6.0, ((0, 8), (1, 4)), jnp.float32)
    column_slab_a = normal_values(arg_keys[6], (OWNERS, SLAB_LEN, W), 1.0, 6.0, ((0, 8), (1, 4)), jnp.float32)
    column_slab_b = normal_values(arg_keys[7], (OWNERS, SLAB_LEN, W), 1.0, 6.0, ((0, 8), (1, 4)), jnp.float32)
    row_live = draw_row_live(jax.random.fold_in(arg_keys[10], 71), 0)
    column_live = draw_column_live(jax.random.fold_in(arg_keys[10], 71), 0)
    return {"left": left, "right": right, "window_a": window_a, "window_b": window_b, "row_slab_a": row_slab_a, "row_slab_b": row_slab_b, "column_slab_a": column_slab_a, "column_slab_b": column_slab_b, "row_live": row_live, "column_live": column_live}


HIGHEST = lax.Precision.HIGHEST


def product(first_matrix, second_matrix):
    return jnp.dot(first_matrix, second_matrix, precision=HIGHEST, preferred_element_type=jnp.float32)


def over_product(first_matrix, second_matrix):
    return lax.dot_general(first_matrix, second_matrix, (((0,), (0,)), ((), ())), precision=HIGHEST, preferred_element_type=jnp.float32)


def reference(left, right, window_a, window_b, row_slab_a, row_slab_b, column_slab_a, column_slab_b, row_live, column_live):
    positions = lax.broadcasted_iota(jnp.int32, (SLAB_LEN, 1), 0)
    carry_a = jnp.zeros((OVL, OVL), jnp.float32)
    carry_b = jnp.zeros((OVL, OVL), jnp.float32)
    windows_a = []
    windows_b = []
    rows_out_a = []
    rows_out_b = []
    columns_out_a = []
    columns_out_b = []
    for owner_index in range(OWNERS):
        left_owner = left[owner_index]
        right_owner = right[owner_index]
        top_left = left_owner[:OVL]
        top_right = right_owner[:OVL]
        updated_a = product(over_product(left_owner, window_a[owner_index]), right_owner) + product(over_product(top_left, carry_a), top_right)
        updated_b = product(over_product(left_owner, window_b[owner_index]), right_owner) + product(over_product(top_left, carry_b), top_right)
        carry_a = updated_a[W - OVL:, W - OVL:]
        carry_b = updated_b[W - OVL:, W - OVL:]
        windows_a.append(updated_a)
        windows_b.append(updated_b)
        row_keep = positions < row_live[owner_index]
        column_keep = positions < column_live[owner_index]
        rows_out_a.append(jnp.where(row_keep, product(row_slab_a[owner_index], left_owner), row_slab_a[owner_index]))
        rows_out_b.append(jnp.where(row_keep, product(row_slab_b[owner_index], left_owner), row_slab_b[owner_index]))
        columns_out_a.append(jnp.where(column_keep, product(column_slab_a[owner_index], right_owner), column_slab_a[owner_index]))
        columns_out_b.append(jnp.where(column_keep, product(column_slab_b[owner_index], right_owner), column_slab_b[owner_index]))
    return (jnp.stack(windows_a), jnp.stack(windows_b), jnp.stack(rows_out_a), jnp.stack(rows_out_b), jnp.stack(columns_out_a), jnp.stack(columns_out_b))
```

```python
import functools

import jax
import jax.numpy as jnp
from jax import lax
from jax.experimental import pallas as pl
from jax.experimental.pallas import tpu as pltpu
from jax.sharding import PartitionSpec as P

OVL = 256
MESH = pl.DeviceIdType.MESH
F32 = jnp.float32
BF16 = jnp.bfloat16


def split(x):
    high = x.astype(BF16)
    low = (x - high.astype(F32)).astype(BF16)
    return high, low


def mm(a, b):
    return lax.dot_general(a, b, (((1,), (0,)), ((), ())), preferred_element_type=F32)


def mm3(a, b):
    return mm(a[0], b[0]) + (mm(a[0], b[1]) + mm(a[1], b[0]))


def kernel(owners, slabs, copies, *refs):
    (
        row_live, col_live, left, right, wa, wb, rsa, rsb, csa, csb,
        out_w, out_ra, out_rb, out_ca, out_cb,
        lt, rt, waf, wbf, edge_rows, slab_in, slab_out, win_out,
        part, part_in, chip_sum, other_sum, b_half,
        corner, corner_prev, b_prev, c_in, c_out, even_in, k_own, k_other,
        rt_h, rt_l, lt_h, lt_l, lp_h, lp_l,
        load_sem, own_sem, out_sem,
        send_sem, recv_sem,
    ) = refs
    d = lax.axis_index("diag")
    s = lax.axis_index("slab")
    q, c = lax.div(s, 2), lax.rem(s, 2)
    chips = slabs // 2
    mate = q * 2 + (1 - c)
    share, order = left.shape
    tiles = order // OVL
    last = tiles - 1
    cut = order - OVL
    half = OVL // 2
    kind = lax.rem(q, 2)
    odd = lax.rem(d, 2) == 1
    even = lax.rem(d, 2) == 0
    has_next = odd & (d + 2 < owners)
    has_prev = odd & (d >= 2)
    counter = iter(range(copies))

    def copy(i, src, dst, dev):
        return pltpu.make_async_remote_copy(
            src_ref=src, dst_ref=dst, send_sem=send_sem.at[i], recv_sem=recv_sem.at[i],
            device_id=dev, device_id_type=MESH)

    def chip(step):
        return lax.rem(q + step + chips, chips)

    def load(i, src, dst):
        cp = pltpu.make_async_copy(src, dst, load_sem.at[i])
        cp.start()
        return cp

    load_edge = load(0, left.at[:, pl.ds(cut, OVL)], edge_rows)
    loads = [load(1 + i, ref, slab_in.at[i]) for i, ref in enumerate((rsa, rsb, csa, csb))]

    barrier = pltpu.get_barrier_semaphore()

    def greet(dev):
        pl.semaphore_signal(barrier, inc=1, device_id=dev, device_id_type=MESH)

    pair = d + 1 - 2 * lax.rem(d, 2)
    greet((d, mate))
    for step in range(1, chips):
        greet((d, chip(step) * 2 + c))
    greet((pair, s))

    @pl.when(has_next)
    def _():
        greet((d + 2, s))

    @pl.when(has_prev)
    def _():
        greet((d - 2, s))

    sends = []

    class Gather:
        def __init__(self, index, src, buf):
            self.src, self.buf = src, buf
            self.ids = [next(counter) for _ in range(2 * chips - 1)]
            self.own = pltpu.make_async_copy(src, buf.at[s], own_sem.at[index])
            self.own.start()

        def start(self):
            for step in range(1, chips):
                cp = copy(self.ids[step], self.src, self.buf.at[s], (d, chip(step) * 2 + c))
                cp.start()
                sends.append(cp)
            cp = copy(self.ids[0], self.src, self.buf.at[s], (d, mate))
            cp.start()
            sends.append(cp)

        def relay(self):
            for step in range(1, chips):
                slot = chip(-step) * 2 + c
                copy(self.ids[step], self.src, self.buf.at[slot], (d, mate)).wait_recv()
                cp = copy(self.ids[chips + step - 1], self.buf.at[slot], self.buf.at[slot], (d, mate))
                cp.start()
                sends.append(cp)

        def finish(self, own=True):
            if own:
                self.own.wait()
            copy(self.ids[0], self.src, self.buf.at[mate], (d, mate)).wait_recv()
            for step in range(1, chips):
                slot = chip(-step) * 2 + 1 - c
                copy(self.ids[chips + step - 1], self.src, self.buf.at[slot], (d, mate)).wait_recv()

    g_wa = Gather(0, wa, waf)
    g_wb = Gather(1, wb, wbf)
    g_r = [Gather(2 + j, right.at[:, pl.ds(j * OVL, OVL)], rt.at[j]) for j in range(tiles)]
    g_l = [Gather(2 + tiles + j, left.at[:, pl.ds(j * OVL, OVL)], lt.at[j]) for j in range(tiles)]

    def tile(buf, j):
        return buf[j].reshape(order, OVL)

    pl.semaphore_wait(
        barrier, chips + 1 + has_next.astype(jnp.int32) + has_prev.astype(jnp.int32))
    g_r[last].start()
    g_l[last].start()
    g_l[0].start()
    load_edge.wait()
    own_left = split(edge_rows[...].T)
    g_wa.own.wait()
    g_wb.own.wait()
    win = [split(waf[s]), split(wbf[s])]
    g_r[last].relay()
    g_r[last].finish()
    rt_h[last], rt_l[last] = split(tile(rt, last))
    for m in range(2):
        inner = mm3(win[m], (rt_h[last], rt_l[last]))
        block = mm3(own_left, split(inner))
        part[0, m] = block[:half]
        part[1, m] = block[half:]
    i = next(counter)
    on_chip = copy(i, part.at[1 - c], part_in, (d, mate))
    on_chip.start()
    sends.append(on_chip)
    g_l[last].relay()
    on_chip.wait_recv()
    chip_sum[...] = part[c] + part_in[...]
    cross = []
    for step in range(1, chips):
        to = chip(step)
        cp = copy(next(counter), chip_sum.at[lax.rem(to, 2)], other_sum.at[step - 1], (d, to * 2 + c))
        cp.start()
        sends.append(cp)
        cross.append(cp)
    for g in g_l[1:last] + g_r[:last]:
        g.start()
    g_wa.start()
    g_wb.start()
    g_l[last].finish()
    corner[0] = tile(lt, last)[:OVL]
    corner[1] = tile(rt, last)[:OVL]
    i_corner, i_corner2, i_b, i_b2 = [next(counter) for _ in range(4)]

    def corner_copy():
        return copy(i_corner, corner.at[c], corner_prev.at[c], (pair, s))

    def b_copy():
        return copy(i_b, b_half, b_prev.at[c], (pair, s))

    @pl.when(even)
    def _():
        corner_copy().start()

    total = chip_sum[kind]
    for step in range(1, chips):
        cross[step - 1].wait_recv()
        total = total + other_sum[step - 1]
    b_half[...] = total

    @pl.when(even)
    def _():
        b_copy().start()

    i_c, i_c2, i_e, i_e2, i_k, i_k2 = [next(counter) for _ in range(6)]

    def relay_copy(i, buf):
        return copy(i, buf.at[c], buf.at[c], (d, mate))

    def relay_wait(i, buf):
        copy(i, buf.at[c], buf.at[1 - c], (d, mate)).wait_recv()

    def to_even():
        return copy(i_e, c_in.at[c], even_in.at[c], (pair, s))

    def to_next():
        return copy(i_c, c_out, c_in.at[c], (d + 2, s))

    @pl.when(odd)
    def _():
        own_left = corner[0].T
        own_left = split(jnp.where(c == 0, own_left[:half], own_left[half:]))
        own_right = split(corner[1])
        corner_copy().wait_recv()
        relay_copy(i_corner2, corner_prev).start()
        relay_wait(i_corner2, corner_prev)
        prev_left = split(corner_prev[0].T)
        prev_right = split(corner_prev[1])
        step_left = split(mm3(own_left, prev_left))
        step_right = split(mm3(prev_right, own_right))
        b_copy().wait_recv()
        relay_copy(i_b2, b_prev).start()
        relay_wait(i_b2, b_prev)
        k_own[...] = b_prev[...]
        inner = mm3(own_left, split(b_prev[...].reshape(OVL, OVL)))
        step_b = b_half[...] + mm3(split(inner), own_right)

        @pl.when(d < 2)
        def _():
            c_out[...] = step_b

        @pl.when(has_prev)
        def _():
            to_next().wait_recv()
            relay_copy(i_c2, c_in).start()
            to_even().start()
            relay_wait(i_c2, c_in)
            incoming = split(c_in[...].reshape(OVL, OVL))

            @pl.when(has_next)
            def _():
                c_out[...] = step_b + mm3(split(mm3(step_left, incoming)), step_right)
                to_next().start()

            inner = mm3(split(mm3(prev_left, incoming)), prev_right)
            k_own[...] = k_own[...] + inner.reshape(2, half, OVL)

        @pl.when(has_next & (d < 2))
        def _():
            to_next().start()

    @pl.when(d == 0)
    def _():
        k_own[...] = jnp.zeros_like(k_own)

    @pl.when(even & (d >= 2))
    def _():
        to_even().wait_recv()
        relay_copy(i_e2, even_in).start()
        relay_wait(i_e2, even_in)
        k_own[...] = even_in[...]

    k_copy = copy(i_k, k_own.at[c], k_other.at[c], (d, (q + 1 - 2 * kind) * 2 + c))
    k_copy.start()
    sends.append(k_copy)

    results = []

    def slab_pair(first, outs, live, high, low):
        n = slab_in.shape[1]
        keep = s * n + lax.broadcasted_iota(jnp.int32, (n, 1), 0) < live[0]
        for i in (first, first + 1):
            loads[i].wait()
            lhs = split(slab_in[i])
            for j in range(tiles):
                columns = slice(j * OVL, (j + 1) * OVL)
                value = mm3(lhs, (high[j], low[j]))
                slab_out[i, :, columns] = jnp.where(keep, value, slab_in[i, :, columns])
            cp = pltpu.make_async_copy(slab_out.at[i], outs[i - first], out_sem.at[i])
            cp.start()
            results.append(cp)

    for j in range(last):
        g_l[j].relay()
    for j in range(last):
        g_l[j].finish()
    for j in range(tiles):
        lt_h[j], lt_l[j] = split(tile(lt, j))
    slab_pair(0, (out_ra, out_rb), row_live, lt_h, lt_l)
    for index in range(slabs):

        @pl.when(s == index)
        def _():
            begin, end = index * share, (index + 1) * share
            low, high = begin // OVL, -(-end // OVL)
            pieces = [tile(lt, j) for j in range(low, high)]
            block = pieces[0] if len(pieces) == 1 else jnp.concatenate(pieces, axis=1)
            start = begin // 128 * 128 - low * OVL
            stop = -(-end // 128) * 128 - low * OVL
            offset = begin - low * OVL - start
            rows = block[:, start:stop].T[offset:offset + share]
            lp_h[...], lp_l[...] = split(rows)

    for j in range(last):
        g_r[j].relay()
    for j in range(last):
        g_r[j].finish()
    for j in range(last):
        rt_h[j], rt_l[j] = split(tile(rt, j))
    slab_pair(2, (out_ca, out_cb), col_live, rt_h, rt_l)

    lhs = (lp_h[...], lp_l[...])
    for m, (g, buf) in enumerate(((g_wa, waf), (g_wb, wbf))):
        g.relay()
        g.finish(own=False)
        full = buf[...].reshape(order, order)
        x = [mm3(lhs, split(full[:, j * OVL:(j + 1) * OVL])) for j in range(tiles)]
        x = split(jnp.concatenate(x, axis=1))
        for j in range(tiles):
            win_out[m, :, j * OVL:(j + 1) * OVL] = mm3(x, (rt_h[j], rt_l[j]))
    top = (lp_h[:, :OVL], lp_l[:, :OVL])

    def add_carry(m, carry):
        x = split(mm3(top, split(carry[...].reshape(OVL, OVL))))
        for j in range(tiles):
            columns = slice(j * OVL, (j + 1) * OVL)
            win_out[m, :, columns] = win_out[m, :, columns] + mm3(x, (rt_h[j, :OVL], rt_l[j, :OVL]))
        cp = pltpu.make_async_copy(win_out.at[m], out_w.at[m], out_sem.at[4 + len(results) % 2])
        cp.start()
        results.append(cp)

    add_carry(kind, k_own)
    k_copy.wait_recv()
    relay = relay_copy(i_k2, k_other)
    relay.start()
    sends.append(relay)
    relay_wait(i_k2, k_other)
    add_carry(1 - kind, k_other)
    for cp in results:
        cp.wait()

    for cp in sends:
        cp.wait_send()

    @pl.when(even)
    def _():
        corner_copy().wait_send()
        b_copy().wait_send()

    @pl.when(odd)
    def _():
        relay_copy(i_corner2, corner_prev).wait_send()
        relay_copy(i_b2, b_prev).wait_send()

    @pl.when(has_prev)
    def _():
        relay_copy(i_c2, c_in).wait_send()
        to_even().wait_send()

    @pl.when(has_next)
    def _():
        to_next().wait_send()

    @pl.when(even & (d >= 2))
    def _():
        relay_copy(i_e2, even_in).wait_send()


def write_out(*refs):
    windows, slabs, outs, held, sem = refs[0], refs[1:5], refs[5:11], refs[11:17], refs[17]
    ins = (windows.at[0], windows.at[1], *slabs)
    reads = [pltpu.make_async_copy(a, b, sem.at[0, i]) for i, (a, b) in enumerate(zip(ins, held))]
    writes = [pltpu.make_async_copy(a, b, sem.at[1, i]) for i, (a, b) in enumerate(zip(held, outs))]
    for cp in reads:
        cp.start()
    for read, write in zip(reads, writes):
        read.wait()
        write.start()
    for cp in writes:
        cp.wait()


def many_chips(left, right, wa, wb, rsa, rsb, csa, csb, row_live, column_live):
    owners, slabs = lax.axis_size("diag"), lax.axis_size("slab")
    chips = slabs // 2
    share, order = left.shape[1:]
    cut = order - OVL
    half = OVL // 2
    n = rsa.shape[1]
    tiles = order // OVL
    copies = (2 + 2 * tiles) * (2 * chips - 1) + 1 + (chips - 1) + 4 + 6
    smem = pl.BlockSpec(memory_space=pltpu.SMEM)
    hbm = pl.BlockSpec(memory_space=pltpu.HBM)
    win = jax.ShapeDtypeStruct((share, order), F32)
    slab = jax.ShapeDtypeStruct((n, order), F32)
    pair = pltpu.VMEM((2, half, OVL), F32)
    square = pltpu.VMEM((2, OVL, OVL), F32)
    factor = pltpu.VMEM((tiles, slabs, share, OVL), F32)
    window = pltpu.VMEM((slabs, share, order), F32)
    packed = pltpu.VMEM((tiles, order, OVL), BF16)
    outs = pl.pallas_call(
        functools.partial(kernel, owners, slabs, copies),
        out_shape=(jax.ShapeDtypeStruct((2, share, order), F32), slab, slab, slab, slab),
        in_specs=[smem] * 2 + [hbm] * 8,
        out_specs=(hbm,) * 5,
        scratch_shapes=[
            factor, factor, window, window,
            pltpu.VMEM((share, OVL), F32),
            pltpu.VMEM((4, n, order), F32),
            pltpu.VMEM((4, n, order), F32),
            pltpu.VMEM((2, share, order), F32),
            pltpu.VMEM((2, 2, half, OVL), F32),
            pair, pair,
            pltpu.VMEM((chips - 1, half, OVL), F32),
            pltpu.VMEM((half, OVL), F32),
            square, square, pair, pair,
            pltpu.VMEM((half, OVL), F32),
            pair, pair, pair,
            packed, packed, packed, packed,
            pltpu.VMEM((share, order), BF16),
            pltpu.VMEM((share, order), BF16),
            pltpu.SemaphoreType.DMA((5,)),
            pltpu.SemaphoreType.DMA((2 + 2 * tiles,)),
            pltpu.SemaphoreType.DMA((6,)),
            pltpu.SemaphoreType.DMA((copies,)),
            pltpu.SemaphoreType.DMA((copies,)),
        ],
        compiler_params=pltpu.CompilerParams(
            collective_id=0, has_side_effects=True, vmem_limit_bytes=60 * 1024 * 1024
        ),
    )(row_live, column_live, left[0], right[0], wa[0], wb[0], rsa[0], rsb[0], csa[0], csb[0])
    outs = pl.pallas_call(
        write_out,
        out_shape=(win, win, slab, slab, slab, slab),
        in_specs=[hbm] * 5,
        out_specs=(hbm,) * 6,
        scratch_shapes=[pltpu.VMEM(o.shape, F32) for o in (win, win, slab, slab, slab, slab)] + [pltpu.SemaphoreType.DMA((2, 6))],
    )(*outs)
    return tuple(o[None] for o in outs)


def two_chip_kernel(owners, copies, *refs):
    (
        row_live, col_live, left, right, wa, wb, rsa, rsb, csa, csb,
        out_w, out_s,
        lt, rt, win, slab_in, zl, zt, p_out, p_in,
        ends, base, base_out, trail, c_in, c_out, give, kk,
        rt_h, rt_l, lt_h, lt_l, win_h, win_l, lx_h, lx_l, ld_h, ld_l, ll_h, ll_l, mm_h, mm_l,
        load_sem, own_sem, send_sem, recv_sem,
    ) = refs
    d = lax.axis_index("diag")
    s = lax.axis_index("slab")
    q, c = lax.div(s, 2), lax.rem(s, 2)
    z, x = lax.div(d, 2), lax.rem(d, 2)
    slabs = lt.shape[1]
    share, order = left.shape
    tiles = order // OVL
    last = tiles - 1
    mate = q * 2 + (1 - c)
    across = (1 - q) * 2 + c
    across_mate = (1 - q) * 2 + (1 - c)
    pair = d + 1 - 2 * x
    mine, theirs = 1 - x, x
    has_next = d + 2 < owners
    has_prev = d >= 2
    first_core = c == 0
    counter = iter(range(copies))
    sends, core_sends = [], []

    def copy(i, src, dst, dev):
        return pltpu.make_async_remote_copy(
            src_ref=src, dst_ref=dst, send_sem=send_sem.at[i], recv_sem=recv_sem.at[i],
            device_id=dev, device_id_type=MESH)

    def load(i, src, dst):
        cp = pltpu.make_async_copy(src, dst, load_sem.at[i])
        cp.start()
        return cp

    class Gather:
        def __init__(self, src, buf):
            self.src, self.buf = src, buf
            self.ids = [next(counter) for _ in range(3)]

        def send(self, i, src, slot, dev):
            cp = copy(self.ids[i], src, self.buf.at[slot], (d, dev))
            cp.start()
            sends.append(cp)

        def wait(self, i, slot):
            copy(self.ids[i], self.src, self.buf.at[slot], (d, mate)).wait_recv()

        def to_across(self):
            self.send(0, self.src, s, across)

        def to_mate(self):
            self.send(1, self.src, s, mate)

        def relay(self):
            self.wait(0, across)
            self.send(2, self.buf.at[across], across, mate)

        def from_mate(self):
            self.wait(1, mate)

        def relayed(self):
            self.wait(2, across_mate)

    g_r = [Gather(right.at[:, pl.ds(j * OVL, OVL)], rt.at[j]) for j in range(tiles)]
    g_l = [Gather(left.at[:, pl.ds(j * OVL, OVL)], lt.at[j]) for j in range(tiles)]
    g_z = [Gather(zl.at[m, s], zl.at[m]) for m in range(2)]
    loads = [load(i, ref, win.at[i]) for i, ref in enumerate((wa, wb))]
    own = []
    for j in reversed(range(tiles)):
        for i, g in ((j, g_r[j]), (tiles + j, g_l[j])):
            cp = pltpu.make_async_copy(g.src, g.buf.at[s], own_sem.at[i])
            cp.start()
            own.append(cp)
    loads += [load(2 + i, ref, slab_in.at[i]) for i, ref in enumerate((rsa, rsb, csa, csb))]

    barrier = pltpu.get_barrier_semaphore()

    def greet(dev):
        pl.semaphore_signal(barrier, inc=1, device_id=dev, device_id_type=MESH)

    greet((d, mate))
    greet((d, across))
    greet((pair, s))

    @pl.when(has_next)
    def _():
        greet((d + 2, s))

    @pl.when(has_prev)
    def _():
        greet((d - 2, s))

    pl.semaphore_wait(barrier, 3 + has_next.astype(jnp.int32) + has_prev.astype(jnp.int32))
    g_r[last].to_across()
    g_l[last].to_across()
    for g in (g_r[last], g_l[last], *g_r[:last], *g_l[:last]):
        g.to_mate()

    i_p, i_q, i_b, i_c, i_k, i_m, i_n = [next(counter) for _ in range(7)]
    i_z = [[next(counter) for _ in range(2)] for _ in range(last)]
    i_o = [[next(counter) for _ in range(2)] for _ in range(last)]

    def end_copy(i, k):
        return copy(i, ends.at[x, k], ends.at[x, k], (pair, s))

    def end_wait(i, k):
        copy(i, ends.at[x, k], ends.at[1 - x, k], (pair, s)).wait_recv()

    def tile(buf, j):
        return buf[j].reshape(order, OVL)

    def columns(j):
        return slice(j * OVL, (j + 1) * OVL)

    def turned(begin, chip):
        end = begin + share
        low, high = begin // OVL, -(-end // OVL)
        pieces = [lt[j, 2 * chip:2 * chip + 2].reshape(2 * share, OVL) for j in range(low, high)]
        block = pieces[0] if len(pieces) == 1 else jnp.concatenate(pieces, axis=1)
        start = begin // 128 * 128 - low * OVL
        stop = -(-end // 128) * 128 - low * OVL
        offset = begin - low * OVL - start
        return split(block[:, start:stop].T[offset:offset + share])

    for i in range(2):
        loads[i].wait()
        win_h[i], win_l[i] = split(win[i])
    for cp in own:
        cp.wait()
    for g in g_l:
        g.from_mate()
    for index in range(slabs):

        @pl.when(s == index)
        def _():
            chip = index // 2
            lx_h[chip], lx_l[chip] = turned(index * share, chip)
            ld_h[...], ld_l[...] = turned((index + 2) % slabs * share, chip)

    def factor(g, buf, high, low, j):
        g.relay()
        g.relayed()
        full = tile(buf, j)
        high[j], low[j] = split(full)
        return full

    for g in g_r:
        g.from_mate()
    full = factor(g_r[last], rt, rt_h, rt_l, last)
    for m in range(2):
        zl[m, s] = mm3((win_h[m], win_l[m]), (rt_h[last], rt_l[last]))
        g_z[m].to_across()
        g_z[m].to_mate()
    for g in g_r[:last] + g_l[:last]:
        g.to_across()

    @pl.when(first_core)
    def _():
        ends[x, 1] = rt[last].reshape(order, OVL)[:OVL]
        end_copy(i_q, 1).start()

    factor(g_l[last], lt, lt_h, lt_l, last)

    @pl.when(first_core)
    def _():
        full = tile(lt, last)
        ends[x, 0] = full[:OVL]
        end_copy(i_p, 0).start()
        ll_h[...], ll_l[...] = split(full.T)

    n = slab_in.shape[1]
    positions = s * n + lax.broadcasted_iota(jnp.int32, (n, 1), 0)
    for i in range(4):
        loads[2 + i].wait()

    def slab_pair(first, live, high, low, j):
        keep = positions < live[0]
        for i in (first, first + 1):
            value = mm3(split(slab_in[i]), (high[j], low[j]))
            out_s[i, :, columns(j)] = jnp.where(keep, value, slab_in[i, :, columns(j)])

    slab_pair(0, row_live, lt_h, lt_l, last)
    slab_pair(2, col_live, rt_h, rt_l, last)

    PE, QE, PO, QO, MT, NN = range(6)

    def held(i):
        return mm_h[i], mm_l[i]

    def hold(i, value):
        mm_h[i], mm_l[i] = split(value)

    @pl.when(first_core)
    def _():
        end_wait(i_q, 1)
        end_wait(i_p, 0)
        hold(PE, ends[0, 0].T)
        hold(QE, ends[0, 1])
        hold(PO, ends[1, 0].T)
        hold(QO, ends[1, 1])
        hold(MT, mm3(held(PO), held(PE)))
        hold(NN, mm3(held(QE), held(QO)))

    for g in g_z:
        g.relay()
    for g in g_z:
        g.from_mate()
        g.relayed()

    def base_copy():
        return copy(i_b, base_out, base.at[x], (pair, s))

    @pl.when(first_core)
    def _():
        lhs = (ll_h[...], ll_l[...])
        base_out[...] = mm3(lhs, split(zl[theirs].reshape(order, OVL)))
        base_copy().start()
        base[x] = mm3(lhs, split(zl[mine].reshape(order, OVL)))

    def chain_copy():
        return copy(i_c, c_out, c_in, (d + 2, s))

    def pair_copy():
        return copy(i_k, give, kk.at[mine], (pair, s))

    def mate_copy(i, m):
        return copy(i, kk.at[m], kk.at[m], (d, mate))

    def settle(incoming, inside):
        give[...] = jnp.where(x == 1, incoming, inside)
        kk[mine] = jnp.where(x == 1, inside, incoming)
        pair_copy().start()
        mate_copy(i_m, mine).start()

    def chain_first():
        @pl.when(first_core)
        def _():
            copy(i_b, base_out, base.at[1 - x], (pair, s)).wait_recv()
            inner = mm3(held(PO), split(base[0]))
            total = base[1] + mm3(split(inner), held(QO))
            trail[...] = total

            @pl.when((z == 0) & has_next)
            def _():
                c_out[...] = total
                chain_copy().start()

            @pl.when(z == 0)
            def _():
                settle(jnp.zeros_like(total), base[0])

    def chain_step(when):
        @pl.when(first_core & when)
        def _():
            copy(i_c, c_out, c_in, (d - 2, s)).wait_recv()
            incoming = split(c_in[...])

            @pl.when(has_next)
            def _():
                c_out[...] = trail[...] + mm3(held(MT), split(mm3(incoming, held(NN))))
                chain_copy().start()

            settle(c_in[...], base[0] + mm3(held(PE), split(mm3(incoming, held(QE)))))

    for j in range(last):
        factor(g_r[j], rt, rt_h, rt_l, j)
        for m in range(2):
            zt[j, m, c] = mm3((win_h[m], win_l[m]), (rt_h[j], rt_l[j]))
            cp = copy(i_z[j][m], zt.at[j, m, c], zt.at[j, m, c], (d, mate))
            cp.start()
            sends.append(cp)
        slab_pair(2, col_live, rt_h, rt_l, j)
        for m in range(2):
            copy(i_z[j][m], zt.at[j, m, c], zt.at[j, m, 1 - c], (d, mate)).wait_recv()
        for m in range(2):
            rhs = split(zt[j, m].reshape(2 * share, OVL))
            p_out[j, m] = mm3((ld_h[...], ld_l[...]), rhs)
            cp = copy(i_o[j][m], p_out.at[j, m], p_in.at[j, m], (d, across))
            cp.start()
            sends.append(cp)
            out_w[m, :, columns(j)] = mm3((lx_h[q], lx_l[q]), rhs)
        if j == 0:
            chain_first()
    chain_step(z == 1)
    for j in range(last):
        factor(g_l[j], lt, lt_h, lt_l, j)
        slab_pair(0, row_live, lt_h, lt_l, j)
        if j == 0:
            chain_step(z == 2)
    for index in range(slabs):

        @pl.when(s == index)
        def _():
            chip = 1 - index // 2
            lx_h[chip], lx_l[chip] = turned(index * share, chip)

    for m in range(2):
        value = [
            mm3((lx_h[k], lx_l[k]), split(zl[m, 2 * k:2 * k + 2].reshape(2 * share, OVL)))
            for k in range(2)
        ]
        out_w[m, :, columns(last)] = value[0] + value[1]
    chain_step(z >= 3)

    @pl.when(first_core)
    def _():
        copy(i_k, give, kk.at[theirs], (pair, s)).wait_recv()
        mate_copy(i_n, theirs).start()

    @pl.when(c == 1)
    def _():
        mate_copy(i_m, mine).wait_recv()
        mate_copy(i_n, theirs).wait_recv()

    top = (lx_h[0, :, :OVL], lx_l[0, :, :OVL])
    for m in range(2):
        value = split(mm3(top, split(kk[m])))
        for j in range(tiles):
            out_w[m, :, columns(j)] = (
                out_w[m, :, columns(j)] + mm3(value, (rt_h[j, :OVL], rt_l[j, :OVL])))
    for j in range(last):
        for m in range(2):
            copy(i_o[j][m], p_out.at[j, m], p_in.at[j, m], (d, across)).wait_recv()
            out_w[m, :, columns(j)] = out_w[m, :, columns(j)] + p_in[j, m]

    for cp in sends:
        cp.wait_send()

    @pl.when(first_core)
    def _():
        end_copy(i_q, 1).wait_send()
        end_copy(i_p, 0).wait_send()
        base_copy().wait_send()
        pair_copy().wait_send()
        mate_copy(i_m, mine).wait_send()
        mate_copy(i_n, theirs).wait_send()

        @pl.when(has_next)
        def _():
            chain_copy().wait_send()


def put_out(windows, slabs, *refs):
    outs, sem = refs[:6], refs[6]
    held = (windows.at[0], windows.at[1], *[slabs.at[i] for i in range(4)])
    writes = [pltpu.make_async_copy(a, b, sem.at[i]) for i, (a, b) in enumerate(zip(held, outs))]
    for cp in writes[2:] + writes[:2]:
        cp.start()
    for cp in writes:
        cp.wait()


def two_chips(left, right, wa, wb, rsa, rsb, csa, csb, row_live, column_live):
    owners, slabs = lax.axis_size("diag"), lax.axis_size("slab")
    share, order = left.shape[1:]
    n = rsa.shape[1]
    tiles = order // OVL
    last = tiles - 1
    copies = 3 * (2 * tiles + 2) + 7 + 4 * last
    smem = pl.BlockSpec(memory_space=pltpu.SMEM)
    hbm = pl.BlockSpec(memory_space=pltpu.HBM)
    vmem = pl.BlockSpec(memory_space=pltpu.VMEM)
    win = jax.ShapeDtypeStruct((share, order), F32)
    slab = jax.ShapeDtypeStruct((n, order), F32)
    factor = pltpu.VMEM((tiles, slabs, share, OVL), F32)
    square = pltpu.VMEM((OVL, OVL), F32)
    squares = pltpu.VMEM((2, OVL, OVL), F32)
    packed = pltpu.VMEM((tiles, order, OVL), BF16)
    parts = pltpu.VMEM((last, 2, share, OVL), F32)
    held = pl.pallas_call(
        functools.partial(two_chip_kernel, owners, copies),
        out_shape=(pltpu.VMEM((2, share, order), F32), pltpu.VMEM((4, n, order), F32)),
        in_specs=[smem] * 2 + [hbm] * 8,
        out_specs=(vmem, vmem),
        scratch_shapes=[
            factor, factor,
            pltpu.VMEM((2, share, order), F32),
            pltpu.VMEM((4, n, order), F32),
            pltpu.VMEM((2, slabs, share, OVL), F32),
            pltpu.VMEM((last, 2, 2, share, OVL), F32),
            parts, parts,
            pltpu.VMEM((2, 2, OVL, OVL), F32),
            squares, square, square, square, square, square, squares,
            packed, packed, packed, packed,
            pltpu.VMEM((2, share, order), BF16), pltpu.VMEM((2, share, order), BF16),
            pltpu.VMEM((2, share, 2 * share), BF16), pltpu.VMEM((2, share, 2 * share), BF16),
            pltpu.VMEM((share, 2 * share), BF16), pltpu.VMEM((share, 2 * share), BF16),
            pltpu.VMEM((OVL, order), BF16), pltpu.VMEM((OVL, order), BF16),
            pltpu.VMEM((6, OVL, OVL), BF16), pltpu.VMEM((6, OVL, OVL), BF16),
            pltpu.SemaphoreType.DMA((6,)),
            pltpu.SemaphoreType.DMA((2 * tiles,)),
            pltpu.SemaphoreType.DMA((copies,)),
            pltpu.SemaphoreType.DMA((copies,)),
        ],
        compiler_params=pltpu.CompilerParams(
            collective_id=0, has_side_effects=True, vmem_limit_bytes=44 * 1024 * 1024
        ),
    )(row_live, column_live, left[0], right[0], wa[0], wb[0], rsa[0], rsb[0], csa[0], csb[0])
    outs = pl.pallas_call(
        put_out,
        out_shape=(win, win, slab, slab, slab, slab),
        in_specs=[vmem] * 2,
        out_specs=(hbm,) * 6,
        scratch_shapes=[pltpu.SemaphoreType.DMA((6,))],
    )(*held)
    return tuple(o[None] for o in outs)


def solution(mesh):
    block = P("diag", "slab", None)

    def shards(*args):
        fits = lax.axis_size("slab") == 4 and lax.axis_size("diag") % 2 == 0
        return (two_chips if fits else many_chips)(*args)

    return jax.shard_map(
        shards, mesh=mesh, in_specs=(block,) * 8 + (P("diag"),) * 2,
        out_specs=(block,) * 6, check_vma=False)
```

```python
import functools

import jax
import jax.numpy as jnp
from jax import lax
from jax.experimental import pallas as pl
from jax.experimental.pallas import tpu as pltpu
from jax.sharding import PartitionSpec as P

OVL = 256
MESH = pl.DeviceIdType.MESH
F32 = jnp.float32
BF16 = jnp.bfloat16


def split(x):
    high = x.astype(BF16)
    low = (x - high.astype(F32)).astype(BF16)
    return high, low


def mm(a, b):
    return lax.dot_general(a, b, (((1,), (0,)), ((), ())), preferred_element_type=F32)


def mm3(a, b):
    return mm(a[0], b[0]) + (mm(a[0], b[1]) + mm(a[1], b[0]))


def kernel(owners, slabs, copies, *refs):
    (
        row_live, col_live, left, right, wa, wb, rsa, rsb, csa, csb,
        out_w, out_ra, out_rb, out_ca, out_cb,
        lt, rt, waf, wbf, edge_rows, slab_in, slab_out, win_out,
        part, part_in, chip_sum, other_sum, b_half,
        corner, corner_prev, b_prev, c_in, c_out, even_in, k_own, k_other,
        rt_h, rt_l, lt_h, lt_l, lp_h, lp_l,
        load_sem, own_sem, out_sem,
        send_sem, recv_sem,
    ) = refs
    d = lax.axis_index("diag")
    s = lax.axis_index("slab")
    q, c = lax.div(s, 2), lax.rem(s, 2)
    chips = slabs // 2
    mate = q * 2 + (1 - c)
    share, order = left.shape
    tiles = order // OVL
    last = tiles - 1
    cut = order - OVL
    half = OVL // 2
    kind = lax.rem(q, 2)
    odd = lax.rem(d, 2) == 1
    even = lax.rem(d, 2) == 0
    has_next = odd & (d + 2 < owners)
    has_prev = odd & (d >= 2)
    counter = iter(range(copies))

    def copy(i, src, dst, dev):
        return pltpu.make_async_remote_copy(
            src_ref=src, dst_ref=dst, send_sem=send_sem.at[i], recv_sem=recv_sem.at[i],
            device_id=dev, device_id_type=MESH)

    def chip(step):
        return lax.rem(q + step + chips, chips)

    def load(i, src, dst):
        cp = pltpu.make_async_copy(src, dst, load_sem.at[i])
        cp.start()
        return cp

    load_edge = load(0, left.at[:, pl.ds(cut, OVL)], edge_rows)
    loads = [load(1 + i, ref, slab_in.at[i]) for i, ref in enumerate((rsa, rsb, csa, csb))]

    barrier = pltpu.get_barrier_semaphore()

    def greet(dev):
        pl.semaphore_signal(barrier, inc=1, device_id=dev, device_id_type=MESH)

    pair = d + 1 - 2 * lax.rem(d, 2)
    greet((d, mate))
    for step in range(1, chips):
        greet((d, chip(step) * 2 + c))
    greet((pair, s))

    @pl.when(has_next)
    def _():
        greet((d + 2, s))

    @pl.when(has_prev)
    def _():
        greet((d - 2, s))

    sends = []

    class Gather:
        def __init__(self, index, src, buf):
            self.src, self.buf = src, buf
            self.ids = [next(counter) for _ in range(2 * chips - 1)]
            self.own = pltpu.make_async_copy(src, buf.at[s], own_sem.at[index])
            self.own.start()

        def start(self):
            for step in range(1, chips):
                cp = copy(self.ids[step], self.src, self.buf.at[s], (d, chip(step) * 2 + c))
                cp.start()
                sends.append(cp)
            cp = copy(self.ids[0], self.src, self.buf.at[s], (d, mate))
            cp.start()
            sends.append(cp)

        def relay(self):
            for step in range(1, chips):
                slot = chip(-step) * 2 + c
                copy(self.ids[step], self.src, self.buf.at[slot], (d, mate)).wait_recv()
                cp = copy(self.ids[chips + step - 1], self.buf.at[slot], self.buf.at[slot], (d, mate))
                cp.start()
                sends.append(cp)

        def finish(self, own=True):
            if own:
                self.own.wait()
            copy(self.ids[0], self.src, self.buf.at[mate], (d, mate)).wait_recv()
            for step in range(1, chips):
                slot = chip(-step) * 2 + 1 - c
                copy(self.ids[chips + step - 1], self.src, self.buf.at[slot], (d, mate)).wait_recv()

    g_wa = Gather(0, wa, waf)
    g_wb = Gather(1, wb, wbf)
    g_r = [Gather(2 + j, right.at[:, pl.ds(j * OVL, OVL)], rt.at[j]) for j in range(tiles)]
    g_l = [Gather(2 + tiles + j, left.at[:, pl.ds(j * OVL, OVL)], lt.at[j]) for j in range(tiles)]

    def tile(buf, j):
        return buf[j].reshape(order, OVL)

    pl.semaphore_wait(
        barrier, chips + 1 + has_next.astype(jnp.int32) + has_prev.astype(jnp.int32))
    g_r[last].start()
    g_l[last].start()
    g_l[0].start()
    load_edge.wait()
    own_left = split(edge_rows[...].T)
    g_wa.own.wait()
    g_wb.own.wait()
    win = [split(waf[s]), split(wbf[s])]
    g_r[last].relay()
    g_r[last].finish()
    rt_h[last], rt_l[last] = split(tile(rt, last))
    for m in range(2):
        inner = mm3(win[m], (rt_h[last], rt_l[last]))
        block = mm3(own_left, split(inner))
        part[0, m] = block[:half]
        part[1, m] = block[half:]
    i = next(counter)
    on_chip = copy(i, part.at[1 - c], part_in, (d, mate))
    on_chip.start()
    sends.append(on_chip)
    g_l[last].relay()
    on_chip.wait_recv()
    chip_sum[...] = part[c] + part_in[...]
    cross = []
    for step in range(1, chips):
        to = chip(step)
        cp = copy(next(counter), chip_sum.at[lax.rem(to, 2)], other_sum.at[step - 1], (d, to * 2 + c))
        cp.start()
        sends.append(cp)
        cross.append(cp)
    for g in g_l[1:last] + g_r[:last]:
        g.start()
    g_wa.start()
    g_wb.start()
    g_l[last].finish()
    corner[0] = tile(lt, last)[:OVL]
    corner[1] = tile(rt, last)[:OVL]
    i_corner, i_corner2, i_b, i_b2 = [next(counter) for _ in range(4)]

    def corner_copy():
        return copy(i_corner, corner.at[c], corner_prev.at[c], (pair, s))

    def b_copy():
        return copy(i_b, b_half, b_prev.at[c], (pair, s))

    @pl.when(even)
    def _():
        corner_copy().start()

    total = chip_sum[kind]
    for step in range(1, chips):
        cross[step - 1].wait_recv()
        total = total + other_sum[step - 1]
    b_half[...] = total

    @pl.when(even)
    def _():
        b_copy().start()

    i_c, i_c2, i_e, i_e2, i_k, i_k2 = [next(counter) for _ in range(6)]

    def relay_copy(i, buf):
        return copy(i, buf.at[c], buf.at[c], (d, mate))

    def relay_wait(i, buf):
        copy(i, buf.at[c], buf.at[1 - c], (d, mate)).wait_recv()

    def to_even():
        return copy(i_e, c_in.at[c], even_in.at[c], (pair, s))

    def to_next():
        return copy(i_c, c_out, c_in.at[c], (d + 2, s))

    @pl.when(odd)
    def _():
        own_left = corner[0].T
        own_left = split(jnp.where(c == 0, own_left[:half], own_left[half:]))
        own_right = split(corner[1])
        corner_copy().wait_recv()
        relay_copy(i_corner2, corner_prev).start()
        relay_wait(i_corner2, corner_prev)
        prev_left = split(corner_prev[0].T)
        prev_right = split(corner_prev[1])
        step_left = split(mm3(own_left, prev_left))
        step_right = split(mm3(prev_right, own_right))
        b_copy().wait_recv()
        relay_copy(i_b2, b_prev).start()
        relay_wait(i_b2, b_prev)
        k_own[...] = b_prev[...]
        inner = mm3(own_left, split(b_prev[...].reshape(OVL, OVL)))
        step_b = b_half[...] + mm3(split(inner), own_right)

        @pl.when(d < 2)
        def _():
            c_out[...] = step_b

        @pl.when(has_prev)
        def _():
            to_next().wait_recv()
            relay_copy(i_c2, c_in).start()
            to_even().start()
            relay_wait(i_c2, c_in)
            incoming = split(c_in[...].reshape(OVL, OVL))

            @pl.when(has_next)
            def _():
                c_out[...] = step_b + mm3(split(mm3(step_left, incoming)), step_right)
                to_next().start()

            inner = mm3(split(mm3(prev_left, incoming)), prev_right)
            k_own[...] = k_own[...] + inner.reshape(2, half, OVL)

        @pl.when(has_next & (d < 2))
        def _():
            to_next().start()

    @pl.when(d == 0)
    def _():
        k_own[...] = jnp.zeros_like(k_own)

    @pl.when(even & (d >= 2))
    def _():
        to_even().wait_recv()
        relay_copy(i_e2, even_in).start()
        relay_wait(i_e2, even_in)
        k_own[...] = even_in[...]

    k_copy = copy(i_k, k_own.at[c], k_other.at[c], (d, (q + 1 - 2 * kind) * 2 + c))
    k_copy.start()
    sends.append(k_copy)

    results = []

    def slab_pair(first, outs, live, high, low):
        n = slab_in.shape[1]
        keep = s * n + lax.broadcasted_iota(jnp.int32, (n, 1), 0) < live[0]
        for i in (first, first + 1):
            loads[i].wait()
            lhs = split(slab_in[i])
            for j in range(tiles):
                columns = slice(j * OVL, (j + 1) * OVL)
                value = mm3(lhs, (high[j], low[j]))
                slab_out[i, :, columns] = jnp.where(keep, value, slab_in[i, :, columns])
            cp = pltpu.make_async_copy(slab_out.at[i], outs[i - first], out_sem.at[i])
            cp.start()
            results.append(cp)

    for j in range(last):
        g_l[j].relay()
    for j in range(last):
        g_l[j].finish()
    for j in range(tiles):
        lt_h[j], lt_l[j] = split(tile(lt, j))
    slab_pair(0, (out_ra, out_rb), row_live, lt_h, lt_l)
    for index in range(slabs):

        @pl.when(s == index)
        def _():
            begin, end = index * share, (index + 1) * share
            low, high = begin // OVL, -(-end // OVL)
            pieces = [tile(lt, j) for j in range(low, high)]
            block = pieces[0] if len(pieces) == 1 else jnp.concatenate(pieces, axis=1)
            start = begin // 128 * 128 - low * OVL
            stop = -(-end // 128) * 128 - low * OVL
            offset = begin - low * OVL - start
            rows = block[:, start:stop].T[offset:offset + share]
            lp_h[...], lp_l[...] = split(rows)

    for j in range(last):
        g_r[j].relay()
    for j in range(last):
        g_r[j].finish()
    for j in range(last):
        rt_h[j], rt_l[j] = split(tile(rt, j))
    slab_pair(2, (out_ca, out_cb), col_live, rt_h, rt_l)

    lhs = (lp_h[...], lp_l[...])
    for m, (g, buf) in enumerate(((g_wa, waf), (g_wb, wbf))):
        g.relay()
        g.finish(own=False)
        full = buf[...].reshape(order, order)
        x = [mm3(lhs, split(full[:, j * OVL:(j + 1) * OVL])) for j in range(tiles)]
        x = split(jnp.concatenate(x, axis=1))
        for j in range(tiles):
            win_out[m, :, j * OVL:(j + 1) * OVL] = mm3(x, (rt_h[j], rt_l[j]))
    top = (lp_h[:, :OVL], lp_l[:, :OVL])

    def add_carry(m, carry):
        x = split(mm3(top, split(carry[...].reshape(OVL, OVL))))
        for j in range(tiles):
            columns = slice(j * OVL, (j + 1) * OVL)
            win_out[m, :, columns] = win_out[m, :, columns] + mm3(x, (rt_h[j, :OVL], rt_l[j, :OVL]))
        cp = pltpu.make_async_copy(win_out.at[m], out_w.at[m], out_sem.at[4 + len(results) % 2])
        cp.start()
        results.append(cp)

    add_carry(kind, k_own)
    k_copy.wait_recv()
    relay = relay_copy(i_k2, k_other)
    relay.start()
    sends.append(relay)
    relay_wait(i_k2, k_other)
    add_carry(1 - kind, k_other)
    for cp in results:
        cp.wait()

    for cp in sends:
        cp.wait_send()

    @pl.when(even)
    def _():
        corner_copy().wait_send()
        b_copy().wait_send()

    @pl.when(odd)
    def _():
        relay_copy(i_corner2, corner_prev).wait_send()
        relay_copy(i_b2, b_prev).wait_send()

    @pl.when(has_prev)
    def _():
        relay_copy(i_c2, c_in).wait_send()
        to_even().wait_send()

    @pl.when(has_next)
    def _():
        to_next().wait_send()

    @pl.when(even & (d >= 2))
    def _():
        relay_copy(i_e2, even_in).wait_send()


def write_out(*refs):
    windows, slabs, outs, held, sem = refs[0], refs[1:5], refs[5:11], refs[11:17], refs[17]
    ins = (windows.at[0], windows.at[1], *slabs)
    reads = [pltpu.make_async_copy(a, b, sem.at[0, i]) for i, (a, b) in enumerate(zip(ins, held))]
    writes = [pltpu.make_async_copy(a, b, sem.at[1, i]) for i, (a, b) in enumerate(zip(held, outs))]
    for cp in reads:
        cp.start()
    for read, write in zip(reads, writes):
        read.wait()
        write.start()
    for cp in writes:
        cp.wait()


def many_chips(left, right, wa, wb, rsa, rsb, csa, csb, row_live, column_live):
    owners, slabs = lax.axis_size("diag"), lax.axis_size("slab")
    chips = slabs // 2
    share, order = left.shape[1:]
    cut = order - OVL
    half = OVL // 2
    n = rsa.shape[1]
    tiles = order // OVL
    copies = (2 + 2 * tiles) * (2 * chips - 1) + 1 + (chips - 1) + 4 + 6
    smem = pl.BlockSpec(memory_space=pltpu.SMEM)
    hbm = pl.BlockSpec(memory_space=pltpu.HBM)
    win = jax.ShapeDtypeStruct((share, order), F32)
    slab = jax.ShapeDtypeStruct((n, order), F32)
    pair = pltpu.VMEM((2, half, OVL), F32)
    square = pltpu.VMEM((2, OVL, OVL), F32)
    factor = pltpu.VMEM((tiles, slabs, share, OVL), F32)
    window = pltpu.VMEM((slabs, share, order), F32)
    packed = pltpu.VMEM((tiles, order, OVL), BF16)
    outs = pl.pallas_call(
        functools.partial(kernel, owners, slabs, copies),
        out_shape=(jax.ShapeDtypeStruct((2, share, order), F32), slab, slab, slab, slab),
        in_specs=[smem] * 2 + [hbm] * 8,
        out_specs=(hbm,) * 5,
        scratch_shapes=[
            factor, factor, window, window,
            pltpu.VMEM((share, OVL), F32),
            pltpu.VMEM((4, n, order), F32),
            pltpu.VMEM((4, n, order), F32),
            pltpu.VMEM((2, share, order), F32),
            pltpu.VMEM((2, 2, half, OVL), F32),
            pair, pair,
            pltpu.VMEM((chips - 1, half, OVL), F32),
            pltpu.VMEM((half, OVL), F32),
            square, square, pair, pair,
            pltpu.VMEM((half, OVL), F32),
            pair, pair, pair,
            packed, packed, packed, packed,
            pltpu.VMEM((share, order), BF16),
            pltpu.VMEM((share, order), BF16),
            pltpu.SemaphoreType.DMA((5,)),
            pltpu.SemaphoreType.DMA((2 + 2 * tiles,)),
            pltpu.SemaphoreType.DMA((6,)),
            pltpu.SemaphoreType.DMA((copies,)),
            pltpu.SemaphoreType.DMA((copies,)),
        ],
        compiler_params=pltpu.CompilerParams(
            collective_id=0, has_side_effects=True, vmem_limit_bytes=60 * 1024 * 1024
        ),
    )(row_live, column_live, left[0], right[0], wa[0], wb[0], rsa[0], rsb[0], csa[0], csb[0])
    outs = pl.pallas_call(
        write_out,
        out_shape=(win, win, slab, slab, slab, slab),
        in_specs=[hbm] * 5,
        out_specs=(hbm,) * 6,
        scratch_shapes=[pltpu.VMEM(o.shape, F32) for o in (win, win, slab, slab, slab, slab)] + [pltpu.SemaphoreType.DMA((2, 6))],
    )(*outs)
    return tuple(o[None] for o in outs)


def two_chip_kernel(owners, copies, *refs):
    (
        row_live, col_live, left, right, wa, wb, rsa, rsb, csa, csb,
        out_w, out_s,
        lt, rt, win, slab_in, zl, zt, p_out, p_in,
        ends, base, base_out, trail, c_in, c_out, give, kk,
        rt_h, rt_l, lt_h, lt_l, win_h, win_l, lx_h, lx_l, ld_h, ld_l, ll_h, ll_l, mm_h, mm_l,
        load_sem, own_sem, send_sem, recv_sem,
    ) = refs
    d = lax.axis_index("diag")
    s = lax.axis_index("slab")
    q, c = lax.div(s, 2), lax.rem(s, 2)
    z, x = lax.div(d, 2), lax.rem(d, 2)
    slabs = lt.shape[1]
    share, order = left.shape
    tiles = order // OVL
    last = tiles - 1
    mate = q * 2 + (1 - c)
    across = (1 - q) * 2 + c
    across_mate = (1 - q) * 2 + (1 - c)
    pair = d + 1 - 2 * x
    mine, theirs = 1 - x, x
    has_next = d + 2 < owners
    has_prev = d >= 2
    first_core = c == 0
    counter = iter(range(copies))
    sends, core_sends = [], []

    def copy(i, src, dst, dev):
        return pltpu.make_async_remote_copy(
            src_ref=src, dst_ref=dst, send_sem=send_sem.at[i], recv_sem=recv_sem.at[i],
            device_id=dev, device_id_type=MESH)

    def load(i, src, dst):
        cp = pltpu.make_async_copy(src, dst, load_sem.at[i])
        cp.start()
        return cp

    class Gather:
        def __init__(self, src, buf):
            self.src, self.buf = src, buf
            self.ids = [next(counter) for _ in range(3)]

        def send(self, i, src, slot, dev):
            cp = copy(self.ids[i], src, self.buf.at[slot], (d, dev))
            cp.start()
            sends.append(cp)

        def wait(self, i, slot):
            copy(self.ids[i], self.src, self.buf.at[slot], (d, mate)).wait_recv()

        def to_across(self):
            self.send(0, self.src, s, across)

        def to_mate(self):
            self.send(1, self.src, s, mate)

        def relay(self):
            self.wait(0, across)
            self.send(2, self.buf.at[across], across, mate)

        def from_mate(self):
            self.wait(1, mate)

        def relayed(self):
            self.wait(2, across_mate)

    g_r = [Gather(right.at[:, pl.ds(j * OVL, OVL)], rt.at[j]) for j in range(tiles)]
    g_l = [Gather(left.at[:, pl.ds(j * OVL, OVL)], lt.at[j]) for j in range(tiles)]
    g_z = [Gather(zl.at[m, s], zl.at[m]) for m in range(2)]
    loads = [load(i, ref, win.at[i]) for i, ref in enumerate((wa, wb))]
    own = []
    for j in reversed(range(tiles)):
        for i, g in ((j, g_r[j]), (tiles + j, g_l[j])):
            cp = pltpu.make_async_copy(g.src, g.buf.at[s], own_sem.at[i])
            cp.start()
            own.append(cp)
    loads += [load(2 + i, ref, slab_in.at[i]) for i, ref in enumerate((rsa, rsb, csa, csb))]

    barrier = pltpu.get_barrier_semaphore()

    def greet(dev):
        pl.semaphore_signal(barrier, inc=1, device_id=dev, device_id_type=MESH)

    greet((d, mate))
    greet((d, across))
    greet((pair, s))

    @pl.when(has_next)
    def _():
        greet((d + 2, s))

    @pl.when(has_prev)
    def _():
        greet((d - 2, s))

    pl.semaphore_wait(barrier, 3 + has_next.astype(jnp.int32) + has_prev.astype(jnp.int32))
    g_r[last].to_across()
    g_l[last].to_across()
    for g in (g_r[last], g_l[last], *g_r[:last], *g_l[:last]):
        g.to_mate()

    i_p, i_q, i_b, i_c, i_k, i_m, i_n = [next(counter) for _ in range(7)]
    i_z = [[next(counter) for _ in range(2)] for _ in range(last)]
    i_o = [[next(counter) for _ in range(2)] for _ in range(last)]

    def end_copy(i, k):
        return copy(i, ends.at[x, k], ends.at[x, k], (pair, s))

    def end_wait(i, k):
        copy(i, ends.at[x, k], ends.at[1 - x, k], (pair, s)).wait_recv()

    def tile(buf, j):
        return buf[j].reshape(order, OVL)

    def columns(j):
        return slice(j * OVL, (j + 1) * OVL)

    def turned(begin, chip):
        end = begin + share
        low, high = begin // OVL, -(-end // OVL)
        pieces = [lt[j, 2 * chip:2 * chip + 2].reshape(2 * share, OVL) for j in range(low, high)]
        block = pieces[0] if len(pieces) == 1 else jnp.concatenate(pieces, axis=1)
        start = begin // 128 * 128 - low * OVL
        stop = -(-end // 128) * 128 - low * OVL
        offset = begin - low * OVL - start
        return split(block[:, start:stop].T[offset:offset + share])

    for i in range(2):
        loads[i].wait()
        win_h[i], win_l[i] = split(win[i])
    for cp in own:
        cp.wait()
    for g in g_l:
        g.from_mate()
    for index in range(slabs):

        @pl.when(s == index)
        def _():
            chip = index // 2
            lx_h[chip], lx_l[chip] = turned(index * share, chip)
            ld_h[...], ld_l[...] = turned((index + 2) % slabs * share, chip)

    def factor(g, buf, high, low, j):
        g.relay()
        g.relayed()
        full = tile(buf, j)
        high[j], low[j] = split(full)
        return full

    for g in g_r:
        g.from_mate()
    full = factor(g_r[last], rt, rt_h, rt_l, last)
    for m in range(2):
        zl[m, s] = mm3((win_h[m], win_l[m]), (rt_h[last], rt_l[last]))
        g_z[m].to_across()
        g_z[m].to_mate()
    for g in g_r[:last] + g_l[:last]:
        g.to_across()

    @pl.when(first_core)
    def _():
        ends[x, 1] = rt[last].reshape(order, OVL)[:OVL]
        end_copy(i_q, 1).start()

    factor(g_l[last], lt, lt_h, lt_l, last)

    @pl.when(first_core)
    def _():
        full = tile(lt, last)
        ends[x, 0] = full[:OVL]
        end_copy(i_p, 0).start()
        ll_h[...], ll_l[...] = split(full.T)

    n = slab_in.shape[1]
    positions = s * n + lax.broadcasted_iota(jnp.int32, (n, 1), 0)
    for i in range(4):
        loads[2 + i].wait()

    def slab_pair(first, live, high, low, j):
        keep = positions < live[0]
        for i in (first, first + 1):
            value = mm3(split(slab_in[i]), (high[j], low[j]))
            out_s[i, :, columns(j)] = jnp.where(keep, value, slab_in[i, :, columns(j)])

    slab_pair(0, row_live, lt_h, lt_l, last)
    slab_pair(2, col_live, rt_h, rt_l, last)

    PE, QE, PO, QO, MT, NN = range(6)

    def held(i):
        return mm_h[i], mm_l[i]

    def hold(i, value):
        mm_h[i], mm_l[i] = split(value)

    @pl.when(first_core)
    def _():
        end_wait(i_q, 1)
        end_wait(i_p, 0)
        hold(PE, ends[0, 0].T)
        hold(QE, ends[0, 1])
        hold(PO, ends[1, 0].T)
        hold(QO, ends[1, 1])
        hold(MT, mm3(held(PO), held(PE)))
        hold(NN, mm3(held(QE), held(QO)))

    for g in g_z:
        g.relay()
    for g in g_z:
        g.from_mate()
        g.relayed()

    def base_copy():
        return copy(i_b, base_out, base.at[x], (pair, s))

    @pl.when(first_core)
    def _():
        lhs = (ll_h[...], ll_l[...])
        base_out[...] = mm3(lhs, split(zl[theirs].reshape(order, OVL)))
        base_copy().start()
        base[x] = mm3(lhs, split(zl[mine].reshape(order, OVL)))

    def chain_copy():
        return copy(i_c, c_out, c_in, (d + 2, s))

    def pair_copy():
        return copy(i_k, give, kk.at[mine], (pair, s))

    def mate_copy(i, m):
        return copy(i, kk.at[m], kk.at[m], (d, mate))

    def settle(incoming, inside):
        give[...] = jnp.where(x == 1, incoming, inside)
        kk[mine] = jnp.where(x == 1, inside, incoming)
        pair_copy().start()
        mate_copy(i_m, mine).start()

    def chain_first():
        @pl.when(first_core)
        def _():
            copy(i_b, base_out, base.at[1 - x], (pair, s)).wait_recv()
            inner = mm3(held(PO), split(base[0]))
            total = base[1] + mm3(split(inner), held(QO))
            trail[...] = total

            @pl.when((z == 0) & has_next)
            def _():
                c_out[...] = total
                chain_copy().start()

            @pl.when(z == 0)
            def _():
                settle(jnp.zeros_like(total), base[0])

    def chain_step(when):
        @pl.when(first_core & when)
        def _():
            copy(i_c, c_out, c_in, (d - 2, s)).wait_recv()
            incoming = split(c_in[...])

            @pl.when(has_next)
            def _():
                c_out[...] = trail[...] + mm3(held(MT), split(mm3(incoming, held(NN))))
                chain_copy().start()

            settle(c_in[...], base[0] + mm3(held(PE), split(mm3(incoming, held(QE)))))

    for j in range(last):
        factor(g_r[j], rt, rt_h, rt_l, j)
        for m in range(2):
            zt[j, m, c] = mm3((win_h[m], win_l[m]), (rt_h[j], rt_l[j]))
            cp = copy(i_z[j][m], zt.at[j, m, c], zt.at[j, m, c], (d, mate))
            cp.start()
            sends.append(cp)
        slab_pair(2, col_live, rt_h, rt_l, j)
        for m in range(2):
            copy(i_z[j][m], zt.at[j, m, c], zt.at[j, m, 1 - c], (d, mate)).wait_recv()
        for m in range(2):
            rhs = split(zt[j, m].reshape(2 * share, OVL))
            p_out[j, m] = mm3((ld_h[...], ld_l[...]), rhs)
            cp = copy(i_o[j][m], p_out.at[j, m], p_in.at[j, m], (d, across))
            cp.start()
            sends.append(cp)
            out_w[m, :, columns(j)] = mm3((lx_h[q], lx_l[q]), rhs)
        if j == 0:
            chain_first()
    chain_step(z == 1)
    for j in range(last):
        factor(g_l[j], lt, lt_h, lt_l, j)
        slab_pair(0, row_live, lt_h, lt_l, j)
        if j == 0:
            chain_step(z == 2)
    for index in range(slabs):

        @pl.when(s == index)
        def _():
            chip = 1 - index // 2
            lx_h[chip], lx_l[chip] = turned(index * share, chip)

    for m in range(2):
        value = [
            mm3((lx_h[k], lx_l[k]), split(zl[m, 2 * k:2 * k + 2].reshape(2 * share, OVL)))
            for k in range(2)
        ]
        out_w[m, :, columns(last)] = value[0] + value[1]
    chain_step(z >= 3)

    @pl.when(first_core)
    def _():
        copy(i_k, give, kk.at[theirs], (pair, s)).wait_recv()
        mate_copy(i_n, theirs).start()

    @pl.when(c == 1)
    def _():
        mate_copy(i_m, mine).wait_recv()
        mate_copy(i_n, theirs).wait_recv()

    top = (lx_h[0, :, :OVL], lx_l[0, :, :OVL])
    for m in range(2):
        value = split(mm3(top, split(kk[m])))
        for j in range(tiles):
            out_w[m, :, columns(j)] = (
                out_w[m, :, columns(j)] + mm3(value, (rt_h[j, :OVL], rt_l[j, :OVL])))
    for j in range(last):
        for m in range(2):
            copy(i_o[j][m], p_out.at[j, m], p_in.at[j, m], (d, across)).wait_recv()
            out_w[m, :, columns(j)] = out_w[m, :, columns(j)] + p_in[j, m]

    for cp in sends:
        cp.wait_send()

    @pl.when(first_core)
    def _():
        end_copy(i_q, 1).wait_send()
        end_copy(i_p, 0).wait_send()
        base_copy().wait_send()
        pair_copy().wait_send()
        mate_copy(i_m, mine).wait_send()
        mate_copy(i_n, theirs).wait_send()

        @pl.when(has_next)
        def _():
            chain_copy().wait_send()


def put_out(windows, slabs, *refs):
    outs, sem = refs[:6], refs[6]
    held = (windows.at[0], windows.at[1], *[slabs.at[i] for i in range(4)])
    writes = [pltpu.make_async_copy(a, b, sem.at[i]) for i, (a, b) in enumerate(zip(held, outs))]
    for cp in writes[2:] + writes[:2]:
        cp.start()
    for cp in writes:
        cp.wait()


def two_chips(left, right, wa, wb, rsa, rsb, csa, csb, row_live, column_live):
    owners, slabs = lax.axis_size("diag"), lax.axis_size("slab")
    share, order = left.shape[1:]
    n = rsa.shape[1]
    tiles = order // OVL
    last = tiles - 1
    copies = 3 * (2 * tiles + 2) + 7 + 4 * last
    smem = pl.BlockSpec(memory_space=pltpu.SMEM)
    hbm = pl.BlockSpec(memory_space=pltpu.HBM)
    vmem = pl.BlockSpec(memory_space=pltpu.VMEM)
    win = jax.ShapeDtypeStruct((share, order), F32)
    slab = jax.ShapeDtypeStruct((n, order), F32)
    factor = pltpu.VMEM((tiles, slabs, share, OVL), F32)
    square = pltpu.VMEM((OVL, OVL), F32)
    squares = pltpu.VMEM((2, OVL, OVL), F32)
    packed = pltpu.VMEM((tiles, order, OVL), BF16)
    parts = pltpu.VMEM((last, 2, share, OVL), F32)
    blocks = [
        pltpu.with_memory_space_constraint(a[0], pltpu.HBM)
        for a in (left, right, wa, wb, rsa, rsb, csa, csb)
    ]
    held = pl.pallas_call(
        functools.partial(two_chip_kernel, owners, copies),
        out_shape=(pltpu.VMEM((2, share, order), F32), pltpu.VMEM((4, n, order), F32)),
        in_specs=[smem] * 2 + [hbm] * 8,
        out_specs=(vmem, vmem),
        scratch_shapes=[
            factor, factor,
            pltpu.VMEM((2, share, order), F32),
            pltpu.VMEM((4, n, order), F32),
            pltpu.VMEM((2, slabs, share, OVL), F32),
            pltpu.VMEM((last, 2, 2, share, OVL), F32),
            parts, parts,
            pltpu.VMEM((2, 2, OVL, OVL), F32),
            squares, square, square, square, square, square, squares,
            packed, packed, packed, packed,
            pltpu.VMEM((2, share, order), BF16), pltpu.VMEM((2, share, order), BF16),
            pltpu.VMEM((2, share, 2 * share), BF16), pltpu.VMEM((2, share, 2 * share), BF16),
            pltpu.VMEM((share, 2 * share), BF16), pltpu.VMEM((share, 2 * share), BF16),
            pltpu.VMEM((OVL, order), BF16), pltpu.VMEM((OVL, order), BF16),
            pltpu.VMEM((6, OVL, OVL), BF16), pltpu.VMEM((6, OVL, OVL), BF16),
            pltpu.SemaphoreType.DMA((6,)),
            pltpu.SemaphoreType.DMA((2 * tiles,)),
            pltpu.SemaphoreType.DMA((copies,)),
            pltpu.SemaphoreType.DMA((copies,)),
        ],
        compiler_params=pltpu.CompilerParams(
            collective_id=0, has_side_effects=True, vmem_limit_bytes=44 * 1024 * 1024
        ),
    )(row_live, column_live, *blocks)
    held = [pltpu.with_memory_space_constraint(a, pltpu.VMEM) for a in held]
    outs = pl.pallas_call(
        put_out,
        out_shape=(win, win, slab, slab, slab, slab),
        in_specs=[vmem] * 2,
        out_specs=(hbm,) * 6,
        scratch_shapes=[pltpu.SemaphoreType.DMA((6,))],
    )(*held)
    return tuple(o[None] for o in outs)


def solution(mesh):
    block = P("diag", "slab", None)

    def shards(*args):
        fits = lax.axis_size("slab") == 4 and lax.axis_size("diag") % 2 == 0
        return (two_chips if fits else many_chips)(*args)

    return jax.shard_map(
        shards, mesh=mesh, in_specs=(block,) * 8 + (P("diag"),) * 2,
        out_specs=(block,) * 6, check_vma=False)
```

```python
import functools

import jax
import jax.numpy as jnp
from jax import lax
from jax.experimental import pallas as pl
from jax.experimental.pallas import tpu as pltpu
from jax.sharding import PartitionSpec as P

OVL = 256
MESH = pl.DeviceIdType.MESH
F32 = jnp.float32
BF16 = jnp.bfloat16


def split(x):
    high = x.astype(BF16)
    low = (x - high.astype(F32)).astype(BF16)
    return high, low


def mm(a, b):
    return lax.dot_general(a, b, (((1,), (0,)), ((), ())), preferred_element_type=F32)


def mm3(a, b):
    return mm(a[0], b[0]) + (mm(a[0], b[1]) + mm(a[1], b[0]))


def kernel(owners, slabs, copies, *refs):
    (
        row_live, col_live, left, right, wa, wb, rsa, rsb, csa, csb,
        out_w, out_ra, out_rb, out_ca, out_cb,
        lt, rt, waf, wbf, edge_rows, slab_in, slab_out, win_out,
        part, part_in, chip_sum, other_sum, b_half,
        corner, corner_prev, b_prev, c_in, c_out, even_in, k_own, k_other,
        rt_h, rt_l, lt_h, lt_l, lp_h, lp_l,
        load_sem, own_sem, out_sem,
        send_sem, recv_sem,
    ) = refs
    d = lax.axis_index("diag")
    s = lax.axis_index("slab")
    q, c = lax.div(s, 2), lax.rem(s, 2)
    chips = slabs // 2
    mate = q * 2 + (1 - c)
    share, order = left.shape
    tiles = order // OVL
    last = tiles - 1
    cut = order - OVL
    half = OVL // 2
    kind = lax.rem(q, 2)
    odd = lax.rem(d, 2) == 1
    even = lax.rem(d, 2) == 0
    has_next = odd & (d + 2 < owners)
    has_prev = odd & (d >= 2)
    counter = iter(range(copies))

    def copy(i, src, dst, dev):
        return pltpu.make_async_remote_copy(
            src_ref=src, dst_ref=dst, send_sem=send_sem.at[i], recv_sem=recv_sem.at[i],
            device_id=dev, device_id_type=MESH)

    def chip(step):
        return lax.rem(q + step + chips, chips)

    def load(i, src, dst):
        cp = pltpu.make_async_copy(src, dst, load_sem.at[i])
        cp.start()
        return cp

    load_edge = load(0, left.at[:, pl.ds(cut, OVL)], edge_rows)
    loads = [load(1 + i, ref, slab_in.at[i]) for i, ref in enumerate((rsa, rsb, csa, csb))]

    barrier = pltpu.get_barrier_semaphore()

    def greet(dev):
        pl.semaphore_signal(barrier, inc=1, device_id=dev, device_id_type=MESH)

    pair = d + 1 - 2 * lax.rem(d, 2)
    greet((d, mate))
    for step in range(1, chips):
        greet((d, chip(step) * 2 + c))
    greet((pair, s))

    @pl.when(has_next)
    def _():
        greet((d + 2, s))

    @pl.when(has_prev)
    def _():
        greet((d - 2, s))

    sends = []

    class Gather:
        def __init__(self, index, src, buf):
            self.src, self.buf = src, buf
            self.ids = [next(counter) for _ in range(2 * chips - 1)]
            self.own = pltpu.make_async_copy(src, buf.at[s], own_sem.at[index])
            self.own.start()

        def start(self):
            for step in range(1, chips):
                cp = copy(self.ids[step], self.src, self.buf.at[s], (d, chip(step) * 2 + c))
                cp.start()
                sends.append(cp)
            cp = copy(self.ids[0], self.src, self.buf.at[s], (d, mate))
            cp.start()
            sends.append(cp)

        def relay(self):
            for step in range(1, chips):
                slot = chip(-step) * 2 + c
                copy(self.ids[step], self.src, self.buf.at[slot], (d, mate)).wait_recv()
                cp = copy(self.ids[chips + step - 1], self.buf.at[slot], self.buf.at[slot], (d, mate))
                cp.start()
                sends.append(cp)

        def finish(self, own=True):
            if own:
                self.own.wait()
            copy(self.ids[0], self.src, self.buf.at[mate], (d, mate)).wait_recv()
            for step in range(1, chips):
                slot = chip(-step) * 2 + 1 - c
                copy(self.ids[chips + step - 1], self.src, self.buf.at[slot], (d, mate)).wait_recv()

    g_wa = Gather(0, wa, waf)
    g_wb = Gather(1, wb, wbf)
    g_r = [Gather(2 + j, right.at[:, pl.ds(j * OVL, OVL)], rt.at[j]) for j in range(tiles)]
    g_l = [Gather(2 + tiles + j, left.at[:, pl.ds(j * OVL, OVL)], lt.at[j]) for j in range(tiles)]

    def tile(buf, j):
        return buf[j].reshape(order, OVL)

    pl.semaphore_wait(
        barrier, chips + 1 + has_next.astype(jnp.int32) + has_prev.astype(jnp.int32))
    g_r[last].start()
    g_l[last].start()
    g_l[0].start()
    load_edge.wait()
    own_left = split(edge_rows[...].T)
    g_wa.own.wait()
    g_wb.own.wait()
    win = [split(waf[s]), split(wbf[s])]
    g_r[last].relay()
    g_r[last].finish()
    rt_h[last], rt_l[last] = split(tile(rt, last))
    for m in range(2):
        inner = mm3(win[m], (rt_h[last], rt_l[last]))
        block = mm3(own_left, split(inner))
        part[0, m] = block[:half]
        part[1, m] = block[half:]
    i = next(counter)
    on_chip = copy(i, part.at[1 - c], part_in, (d, mate))
    on_chip.start()
    sends.append(on_chip)
    g_l[last].relay()
    on_chip.wait_recv()
    chip_sum[...] = part[c] + part_in[...]
    cross = []
    for step in range(1, chips):
        to = chip(step)
        cp = copy(next(counter), chip_sum.at[lax.rem(to, 2)], other_sum.at[step - 1], (d, to * 2 + c))
        cp.start()
        sends.append(cp)
        cross.append(cp)
    for g in g_l[1:last] + g_r[:last]:
        g.start()
    g_wa.start()
    g_wb.start()
    g_l[last].finish()
    corner[0] = tile(lt, last)[:OVL]
    corner[1] = tile(rt, last)[:OVL]
    i_corner, i_corner2, i_b, i_b2 = [next(counter) for _ in range(4)]

    def corner_copy():
        return copy(i_corner, corner.at[c], corner_prev.at[c], (pair, s))

    def b_copy():
        return copy(i_b, b_half, b_prev.at[c], (pair, s))

    @pl.when(even)
    def _():
        corner_copy().start()

    total = chip_sum[kind]
    for step in range(1, chips):
        cross[step - 1].wait_recv()
        total = total + other_sum[step - 1]
    b_half[...] = total

    @pl.when(even)
    def _():
        b_copy().start()

    i_c, i_c2, i_e, i_e2, i_k, i_k2 = [next(counter) for _ in range(6)]

    def relay_copy(i, buf):
        return copy(i, buf.at[c], buf.at[c], (d, mate))

    def relay_wait(i, buf):
        copy(i, buf.at[c], buf.at[1 - c], (d, mate)).wait_recv()

    def to_even():
        return copy(i_e, c_in.at[c], even_in.at[c], (pair, s))

    def to_next():
        return copy(i_c, c_out, c_in.at[c], (d + 2, s))

    @pl.when(odd)
    def _():
        own_left = corner[0].T
        own_left = split(jnp.where(c == 0, own_left[:half], own_left[half:]))
        own_right = split(corner[1])
        corner_copy().wait_recv()
        relay_copy(i_corner2, corner_prev).start()
        relay_wait(i_corner2, corner_prev)
        prev_left = split(corner_prev[0].T)
        prev_right = split(corner_prev[1])
        step_left = split(mm3(own_left, prev_left))
        step_right = split(mm3(prev_right, own_right))
        b_copy().wait_recv()
        relay_copy(i_b2, b_prev).start()
        relay_wait(i_b2, b_prev)
        k_own[...] = b_prev[...]
        inner = mm3(own_left, split(b_prev[...].reshape(OVL, OVL)))
        step_b = b_half[...] + mm3(split(inner), own_right)

        @pl.when(d < 2)
        def _():
            c_out[...] = step_b

        @pl.when(has_prev)
        def _():
            to_next().wait_recv()
            relay_copy(i_c2, c_in).start()
            to_even().start()
            relay_wait(i_c2, c_in)
            incoming = split(c_in[...].reshape(OVL, OVL))

            @pl.when(has_next)
            def _():
                c_out[...] = step_b + mm3(split(mm3(step_left, incoming)), step_right)
                to_next().start()

            inner = mm3(split(mm3(prev_left, incoming)), prev_right)
            k_own[...] = k_own[...] + inner.reshape(2, half, OVL)

        @pl.when(has_next & (d < 2))
        def _():
            to_next().start()

    @pl.when(d == 0)
    def _():
        k_own[...] = jnp.zeros_like(k_own)

    @pl.when(even & (d >= 2))
    def _():
        to_even().wait_recv()
        relay_copy(i_e2, even_in).start()
        relay_wait(i_e2, even_in)
        k_own[...] = even_in[...]

    k_copy = copy(i_k, k_own.at[c], k_other.at[c], (d, (q + 1 - 2 * kind) * 2 + c))
    k_copy.start()
    sends.append(k_copy)

    results = []

    def slab_pair(first, outs, live, high, low):
        n = slab_in.shape[1]
        keep = s * n + lax.broadcasted_iota(jnp.int32, (n, 1), 0) < live[0]
        for i in (first, first + 1):
            loads[i].wait()
            lhs = split(slab_in[i])
            for j in range(tiles):
                columns = slice(j * OVL, (j + 1) * OVL)
                value = mm3(lhs, (high[j], low[j]))
                slab_out[i, :, columns] = jnp.where(keep, value, slab_in[i, :, columns])
            cp = pltpu.make_async_copy(slab_out.at[i], outs[i - first], out_sem.at[i])
            cp.start()
            results.append(cp)

    for j in range(last):
        g_l[j].relay()
    for j in range(last):
        g_l[j].finish()
    for j in range(tiles):
        lt_h[j], lt_l[j] = split(tile(lt, j))
    slab_pair(0, (out_ra, out_rb), row_live, lt_h, lt_l)
    for index in range(slabs):

        @pl.when(s == index)
        def _():
            begin, end = index * share, (index + 1) * share
            low, high = begin // OVL, -(-end // OVL)
            pieces = [tile(lt, j) for j in range(low, high)]
            block = pieces[0] if len(pieces) == 1 else jnp.concatenate(pieces, axis=1)
            start = begin // 128 * 128 - low * OVL
            stop = -(-end // 128) * 128 - low * OVL
            offset = begin - low * OVL - start
            rows = block[:, start:stop].T[offset:offset + share]
            lp_h[...], lp_l[...] = split(rows)

    for j in range(last):
        g_r[j].relay()
    for j in range(last):
        g_r[j].finish()
    for j in range(last):
        rt_h[j], rt_l[j] = split(tile(rt, j))
    slab_pair(2, (out_ca, out_cb), col_live, rt_h, rt_l)

    lhs = (lp_h[...], lp_l[...])
    for m, (g, buf) in enumerate(((g_wa, waf), (g_wb, wbf))):
        g.relay()
        g.finish(own=False)
        full = buf[...].reshape(order, order)
        x = [mm3(lhs, split(full[:, j * OVL:(j + 1) * OVL])) for j in range(tiles)]
        x = split(jnp.concatenate(x, axis=1))
        for j in range(tiles):
            win_out[m, :, j * OVL:(j + 1) * OVL] = mm3(x, (rt_h[j], rt_l[j]))
    top = (lp_h[:, :OVL], lp_l[:, :OVL])

    def add_carry(m, carry):
        x = split(mm3(top, split(carry[...].reshape(OVL, OVL))))
        for j in range(tiles):
            columns = slice(j * OVL, (j + 1) * OVL)
            win_out[m, :, columns] = win_out[m, :, columns] + mm3(x, (rt_h[j, :OVL], rt_l[j, :OVL]))
        cp = pltpu.make_async_copy(win_out.at[m], out_w.at[m], out_sem.at[4 + len(results) % 2])
        cp.start()
        results.append(cp)

    add_carry(kind, k_own)
    k_copy.wait_recv()
    relay = relay_copy(i_k2, k_other)
    relay.start()
    sends.append(relay)
    relay_wait(i_k2, k_other)
    add_carry(1 - kind, k_other)
    for cp in results:
        cp.wait()

    for cp in sends:
        cp.wait_send()

    @pl.when(even)
    def _():
        corner_copy().wait_send()
        b_copy().wait_send()

    @pl.when(odd)
    def _():
        relay_copy(i_corner2, corner_prev).wait_send()
        relay_copy(i_b2, b_prev).wait_send()

    @pl.when(has_prev)
    def _():
        relay_copy(i_c2, c_in).wait_send()
        to_even().wait_send()

    @pl.when(has_next)
    def _():
        to_next().wait_send()

    @pl.when(even & (d >= 2))
    def _():
        relay_copy(i_e2, even_in).wait_send()


def write_out(*refs):
    windows, slabs, outs, held, sem = refs[0], refs[1:5], refs[5:11], refs[11:17], refs[17]
    ins = (windows.at[0], windows.at[1], *slabs)
    reads = [pltpu.make_async_copy(a, b, sem.at[0, i]) for i, (a, b) in enumerate(zip(ins, held))]
    writes = [pltpu.make_async_copy(a, b, sem.at[1, i]) for i, (a, b) in enumerate(zip(held, outs))]
    for cp in reads:
        cp.start()
    for read, write in zip(reads, writes):
        read.wait()
        write.start()
    for cp in writes:
        cp.wait()


def many_chips(left, right, wa, wb, rsa, rsb, csa, csb, row_live, column_live):
    owners, slabs = lax.axis_size("diag"), lax.axis_size("slab")
    chips = slabs // 2
    share, order = left.shape[1:]
    cut = order - OVL
    half = OVL // 2
    n = rsa.shape[1]
    tiles = order // OVL
    copies = (2 + 2 * tiles) * (2 * chips - 1) + 1 + (chips - 1) + 4 + 6
    smem = pl.BlockSpec(memory_space=pltpu.SMEM)
    hbm = pl.BlockSpec(memory_space=pltpu.HBM)
    win = jax.ShapeDtypeStruct((share, order), F32)
    slab = jax.ShapeDtypeStruct((n, order), F32)
    pair = pltpu.VMEM((2, half, OVL), F32)
    square = pltpu.VMEM((2, OVL, OVL), F32)
    factor = pltpu.VMEM((tiles, slabs, share, OVL), F32)
    window = pltpu.VMEM((slabs, share, order), F32)
    packed = pltpu.VMEM((tiles, order, OVL), BF16)
    outs = pl.pallas_call(
        functools.partial(kernel, owners, slabs, copies),
        out_shape=(jax.ShapeDtypeStruct((2, share, order), F32), slab, slab, slab, slab),
        in_specs=[smem] * 2 + [hbm] * 8,
        out_specs=(hbm,) * 5,
        scratch_shapes=[
            factor, factor, window, window,
            pltpu.VMEM((share, OVL), F32),
            pltpu.VMEM((4, n, order), F32),
            pltpu.VMEM((4, n, order), F32),
            pltpu.VMEM((2, share, order), F32),
            pltpu.VMEM((2, 2, half, OVL), F32),
            pair, pair,
            pltpu.VMEM((chips - 1, half, OVL), F32),
            pltpu.VMEM((half, OVL), F32),
            square, square, pair, pair,
            pltpu.VMEM((half, OVL), F32),
            pair, pair, pair,
            packed, packed, packed, packed,
            pltpu.VMEM((share, order), BF16),
            pltpu.VMEM((share, order), BF16),
            pltpu.SemaphoreType.DMA((5,)),
            pltpu.SemaphoreType.DMA((2 + 2 * tiles,)),
            pltpu.SemaphoreType.DMA((6,)),
            pltpu.SemaphoreType.DMA((copies,)),
            pltpu.SemaphoreType.DMA((copies,)),
        ],
        compiler_params=pltpu.CompilerParams(
            collective_id=0, has_side_effects=True, vmem_limit_bytes=60 * 1024 * 1024
        ),
    )(row_live, column_live, left[0], right[0], wa[0], wb[0], rsa[0], rsb[0], csa[0], csb[0])
    outs = pl.pallas_call(
        write_out,
        out_shape=(win, win, slab, slab, slab, slab),
        in_specs=[hbm] * 5,
        out_specs=(hbm,) * 6,
        scratch_shapes=[pltpu.VMEM(o.shape, F32) for o in (win, win, slab, slab, slab, slab)] + [pltpu.SemaphoreType.DMA((2, 6))],
    )(*outs)
    return tuple(o[None] for o in outs)


def two_chip_kernel(owners, copies, *refs):
    (
        row_live, col_live, left, right, wa, wb, rsa, rsb, csa, csb,
        out_w, out_s,
        lt, rt, win, slab_in, zl, zt, p_out, p_in,
        ends, base, base_out, trail, c_in, c_out, give, kk,
        rt_h, rt_l, lt_h, lt_l, win_h, win_l, lx_h, lx_l, ld_h, ld_l, ll_h, ll_l, mm_h, mm_l,
        load_sem, own_sem, send_sem, recv_sem,
    ) = refs
    d = lax.axis_index("diag")
    s = lax.axis_index("slab")
    q, c = lax.div(s, 2), lax.rem(s, 2)
    z, x = lax.div(d, 2), lax.rem(d, 2)
    slabs = lt.shape[1]
    share, order = left.shape
    tiles = order // OVL
    last = tiles - 1
    mate = q * 2 + (1 - c)
    across = (1 - q) * 2 + c
    across_mate = (1 - q) * 2 + (1 - c)
    pair = d + 1 - 2 * x
    mine, theirs = 1 - x, x
    has_next = d + 2 < owners
    has_prev = d >= 2
    first_core = c == 0
    counter = iter(range(copies))
    sends = []
    barrier = pltpu.get_barrier_semaphore()

    def greet(dev):
        pl.semaphore_signal(barrier, inc=1, device_id=dev, device_id_type=MESH)

    greet((d, across))
    greet((d, mate))

    @pl.when(first_core)
    def _():
        greet((pair, s))

    @pl.when(first_core & has_next)
    def _():
        greet((d + 2, s))

    @pl.when(first_core & has_prev)
    def _():
        greet((d - 2, s))

    def copy(i, src, dst, dev):
        return pltpu.make_async_remote_copy(
            src_ref=src, dst_ref=dst, send_sem=send_sem.at[i], recv_sem=recv_sem.at[i],
            device_id=dev, device_id_type=MESH)

    def load(i, src, dst):
        cp = pltpu.make_async_copy(src, dst, load_sem.at[i])
        cp.start()
        return cp

    class Gather:
        def __init__(self, src, buf):
            self.src, self.buf = src, buf
            self.ids = [next(counter) for _ in range(3)]

        def send(self, i, src, slot, dev):
            cp = copy(self.ids[i], src, self.buf.at[slot], (d, dev))
            cp.start()
            sends.append(cp)

        def wait(self, i, slot):
            copy(self.ids[i], self.src, self.buf.at[slot], (d, mate)).wait_recv()

        def to_across(self):
            self.send(0, self.src, s, across)

        def to_mate(self):
            self.send(1, self.src, s, mate)

        def relay(self):
            self.wait(0, across)
            self.send(2, self.buf.at[across], across, mate)

        def from_mate(self):
            self.wait(1, mate)

        def relayed(self):
            self.wait(2, across_mate)

    g_r = [Gather(right.at[:, pl.ds(j * OVL, OVL)], rt.at[j]) for j in range(tiles)]
    g_l = [Gather(left.at[:, pl.ds(j * OVL, OVL)], lt.at[j]) for j in range(tiles)]
    g_z = [Gather(zl.at[m, s], zl.at[m]) for m in range(2)]
    around = 1 + has_next.astype(jnp.int32) + has_prev.astype(jnp.int32)
    pl.semaphore_wait(barrier, jnp.where(first_core, 2 + around, 2))
    g_r[last].to_across()
    g_l[last].to_across()
    for g in (g_r[last], g_l[last], *g_r[:last], *g_l[:last]):
        g.to_mate()
    loads = [load(i, ref, win.at[i]) for i, ref in enumerate((wa, wb))]
    own = []
    for j in reversed(range(tiles)):
        for i, g in ((j, g_r[j]), (tiles + j, g_l[j])):
            cp = pltpu.make_async_copy(g.src, g.buf.at[s], own_sem.at[i])
            cp.start()
            own.append(cp)
    loads += [load(2 + i, ref, slab_in.at[i]) for i, ref in enumerate((rsa, rsb, csa, csb))]

    i_p, i_q, i_b, i_c, i_k, i_m, i_n = [next(counter) for _ in range(7)]
    i_z = [[next(counter) for _ in range(2)] for _ in range(last)]
    i_o = [[next(counter) for _ in range(2)] for _ in range(last)]

    def end_copy(i, k):
        return copy(i, ends.at[x, k], ends.at[x, k], (pair, s))

    def end_wait(i, k):
        copy(i, ends.at[x, k], ends.at[1 - x, k], (pair, s)).wait_recv()

    def tile(buf, j):
        return buf[j].reshape(order, OVL)

    def columns(j):
        return slice(j * OVL, (j + 1) * OVL)

    def turned(begin, chip):
        end = begin + share
        low, high = begin // OVL, -(-end // OVL)
        pieces = [lt[j, 2 * chip:2 * chip + 2].reshape(2 * share, OVL) for j in range(low, high)]
        block = pieces[0] if len(pieces) == 1 else jnp.concatenate(pieces, axis=1)
        start = begin // 128 * 128 - low * OVL
        stop = -(-end // 128) * 128 - low * OVL
        offset = begin - low * OVL - start
        return split(block[:, start:stop].T[offset:offset + share])

    for i in range(2):
        loads[i].wait()
        win_h[i], win_l[i] = split(win[i])
    for cp in own:
        cp.wait()
    for g in g_l:
        g.from_mate()
    for index in range(slabs):

        @pl.when(s == index)
        def _():
            chip = index // 2
            lx_h[chip], lx_l[chip] = turned(index * share, chip)
            ld_h[...], ld_l[...] = turned((index + 2) % slabs * share, chip)

    def factor(g, buf, high, low, j):
        g.relayed()
        full = tile(buf, j)
        high[j], low[j] = split(full)
        return full

    for g in g_r:
        g.from_mate()
    g_r[last].relay()
    factor(g_r[last], rt, rt_h, rt_l, last)
    for m in range(2):
        zl[m, s] = mm3((win_h[m], win_l[m]), (rt_h[last], rt_l[last]))
        g_z[m].to_across()
        g_z[m].to_mate()
    for g in g_r[:last] + g_l[:last]:
        g.to_across()

    @pl.when(first_core)
    def _():
        ends[x, 1] = rt[last].reshape(order, OVL)[:OVL]
        end_copy(i_q, 1).start()

    g_l[last].relay()
    factor(g_l[last], lt, lt_h, lt_l, last)

    @pl.when(first_core)
    def _():
        full = tile(lt, last)
        ends[x, 0] = full[:OVL]
        end_copy(i_p, 0).start()
        ll_h[...], ll_l[...] = split(full.T)

    n = slab_in.shape[1]
    positions = s * n + lax.broadcasted_iota(jnp.int32, (n, 1), 0)
    for cp in loads[2:]:
        cp.wait()

    def slab_pair(first, live, high, low, j):
        keep = positions < live[0]
        for i in (first, first + 1):
            value = mm3(split(slab_in[i]), (high[j], low[j]))
            out_s[i, :, columns(j)] = jnp.where(keep, value, slab_in[i, :, columns(j)])

    slab_pair(0, row_live, lt_h, lt_l, last)
    slab_pair(2, col_live, rt_h, rt_l, last)

    PE, QE, PO, QO, MT, NN = range(6)

    def held(i):
        return mm_h[i], mm_l[i]

    def hold(i, value):
        mm_h[i], mm_l[i] = split(value)

    @pl.when(first_core)
    def _():
        end_wait(i_q, 1)
        end_wait(i_p, 0)
        hold(PE, ends[0, 0].T)
        hold(QE, ends[0, 1])
        hold(PO, ends[1, 0].T)
        hold(QO, ends[1, 1])
        hold(MT, mm3(held(PO), held(PE)))
        hold(NN, mm3(held(QE), held(QO)))

    def base_copy():
        return copy(i_b, base_out, base.at[x], (pair, s))

    def chain_copy():
        return copy(i_c, c_out, c_in, (d + 2, s))

    def pair_copy(src):
        return copy(i_k, src, kk.at[mine], (pair, s))

    def mate_copy(i, src, m):
        return copy(i, src, kk.at[m], (d, mate))

    def share_incoming():
        @pl.when(x == 1)
        def _():
            pair_copy(c_in).start()

        @pl.when(x == 0)
        def _():
            mate_copy(i_m, c_in, mine).start()
            kk[mine] = c_in[...]

    def share_inside(inside):
        @pl.when(x == 1)
        def _():
            kk[mine] = inside
            mate_copy(i_m, kk.at[mine], mine).start()

        @pl.when(x == 0)
        def _():
            give[...] = inside
            pair_copy(give).start()

    def chain_first(when):
        @pl.when(first_core & when)
        def _():
            copy(i_b, base_out, base.at[1 - x], (pair, s)).wait_recv()
            inner = mm3(held(PO), split(base[0]))
            total = base[1] + mm3(split(inner), held(QO))
            trail[...] = total

            @pl.when((z == 0) & has_next)
            def _():
                c_out[...] = total
                chain_copy().start()

            @pl.when(z == 0)
            def _():
                c_in[...] = jnp.zeros_like(total)
                share_incoming()
                share_inside(base[0])

    def chain_step(when):
        @pl.when(first_core & when)
        def _():
            copy(i_c, c_out, c_in, (d - 2, s)).wait_recv()
            share_incoming()
            incoming = split(c_in[...])

            @pl.when(has_next)
            def _():
                c_out[...] = trail[...] + mm3(held(MT), split(mm3(incoming, held(NN))))
                chain_copy().start()

            share_inside(base[0] + mm3(held(PE), split(mm3(incoming, held(QE)))))

    for m in range(2):
        g_z[m].relay()
        g_z[m].from_mate()
        g_z[m].relayed()

        @pl.when(first_core)
        def _():
            value = mm3((ll_h[...], ll_l[...]), split(zl[m].reshape(order, OVL)))

            @pl.when(theirs == m)
            def _():
                base_out[...] = value
                base_copy().start()

            @pl.when(mine == m)
            def _():
                base[x] = value

    chain_first(x == 1)
    for j in range(last):
        g_r[j].relay()
        factor(g_r[j], rt, rt_h, rt_l, j)
        for m in range(2):
            zt[j, m, c] = mm3((win_h[m], win_l[m]), (rt_h[j], rt_l[j]))
            cp = copy(i_z[j][m], zt.at[j, m, c], zt.at[j, m, c], (d, mate))
            cp.start()
            sends.append(cp)
        if j == 0:
            chain_first(x == 0)
        if j == last - 1:
            chain_step((x == 0) & (z == 1))
        slab_pair(2, col_live, rt_h, rt_l, j)
        for m in range(2):
            copy(i_z[j][m], zt.at[j, m, c], zt.at[j, m, 1 - c], (d, mate)).wait_recv()
        for m in range(2):
            rhs = split(zt[j, m].reshape(2 * share, OVL))
            p_out[j, m] = mm3((ld_h[...], ld_l[...]), rhs)
            cp = copy(i_o[j][m], p_out.at[j, m], p_in.at[j, m], (d, across))
            cp.start()
            sends.append(cp)
            out_w[m, :, columns(j)] = mm3((lx_h[q], lx_l[q]), rhs)
        if j == 0:
            chain_step((x == 1) & (z == 1))
    chain_step((x == 1) & (z == 2))
    for j in range(last):
        g_l[j].relay()
        factor(g_l[j], lt, lt_h, lt_l, j)
        slab_pair(0, row_live, lt_h, lt_l, j)
        if j == 0:
            chain_step(((x == 1) & (z == 3)) | ((x == 0) & (z == 2)))
    for index in range(slabs):

        @pl.when(s == index)
        def _():
            chip = 1 - index // 2
            lx_h[chip], lx_l[chip] = turned(index * share, chip)

    for m in range(2):
        value = [
            mm3((lx_h[k], lx_l[k]), split(zl[m, 2 * k:2 * k + 2].reshape(2 * share, OVL)))
            for k in range(2)
        ]
        out_w[m, :, columns(last)] = value[0] + value[1]
    chain_step(((x == 1) & (z > 3)) | ((x == 0) & (z >= 3)))

    @pl.when(first_core)
    def _():
        copy(i_k, give, kk.at[theirs], (pair, s)).wait_recv()
        mate_copy(i_n, kk.at[theirs], theirs).start()

    @pl.when(c == 1)
    def _():
        mate_copy(i_m, give, mine).wait_recv()
        mate_copy(i_n, give, theirs).wait_recv()

    top = (lx_h[0, :, :OVL], lx_l[0, :, :OVL])
    for m in range(2):
        value = split(mm3(top, split(kk[m])))
        for j in range(tiles):
            out_w[m, :, columns(j)] = (
                out_w[m, :, columns(j)] + mm3(value, (rt_h[j, :OVL], rt_l[j, :OVL])))
    for j in range(last):
        for m in range(2):
            copy(i_o[j][m], p_out.at[j, m], p_in.at[j, m], (d, across)).wait_recv()
            out_w[m, :, columns(j)] = out_w[m, :, columns(j)] + p_in[j, m]

    for cp in sends:
        cp.wait_send()

    @pl.when(first_core)
    def _():
        end_copy(i_q, 1).wait_send()
        end_copy(i_p, 0).wait_send()
        base_copy().wait_send()
        pair_copy(give).wait_send()
        mate_copy(i_m, give, mine).wait_send()
        mate_copy(i_n, give, theirs).wait_send()

        @pl.when(has_next)
        def _():
            chain_copy().wait_send()


def put_out(windows, slabs, *refs):
    outs, sem = refs[:6], refs[6]
    held = (windows.at[0], windows.at[1], *[slabs.at[i] for i in range(4)])
    writes = [pltpu.make_async_copy(a, b, sem.at[i]) for i, (a, b) in enumerate(zip(held, outs))]
    for cp in writes[2:] + writes[:2]:
        cp.start()
    for cp in writes:
        cp.wait()


def two_chips(left, right, wa, wb, rsa, rsb, csa, csb, row_live, column_live):
    owners, slabs = lax.axis_size("diag"), lax.axis_size("slab")
    share, order = left.shape[1:]
    n = rsa.shape[1]
    tiles = order // OVL
    last = tiles - 1
    copies = 3 * (2 * tiles + 2) + 7 + 4 * last
    hbm = pl.BlockSpec(memory_space=pltpu.HBM)
    vmem = pl.BlockSpec(memory_space=pltpu.VMEM)
    win = jax.ShapeDtypeStruct((share, order), F32)
    slab = jax.ShapeDtypeStruct((n, order), F32)
    factor = pltpu.VMEM((tiles, slabs, share, OVL), F32)
    square = pltpu.VMEM((OVL, OVL), F32)
    squares = pltpu.VMEM((2, OVL, OVL), F32)
    packed = pltpu.VMEM((tiles, order, OVL), BF16)
    parts = pltpu.VMEM((last, 2, share, OVL), F32)
    blocks = [
        pltpu.with_memory_space_constraint(a[0], pltpu.HBM)
        for a in (left, right, wa, wb, rsa, rsb, csa, csb)
    ]
    held = pl.pallas_call(
        functools.partial(two_chip_kernel, owners, copies),
        out_shape=(pltpu.VMEM((2, share, order), F32), pltpu.VMEM((4, n, order), F32)),
        in_specs=[pl.BlockSpec(memory_space=pltpu.SMEM)] * 2 + [hbm] * 8,
        out_specs=(vmem, vmem),
        scratch_shapes=[
            factor, factor,
            pltpu.VMEM((2, share, order), F32),
            pltpu.VMEM((4, n, order), F32),
            pltpu.VMEM((2, slabs, share, OVL), F32),
            pltpu.VMEM((last, 2, 2, share, OVL), F32),
            parts, parts,
            pltpu.VMEM((2, 2, OVL, OVL), F32),
            squares, square, square, square, square, square, squares,
            packed, packed, packed, packed,
            pltpu.VMEM((2, share, order), BF16), pltpu.VMEM((2, share, order), BF16),
            pltpu.VMEM((2, share, 2 * share), BF16), pltpu.VMEM((2, share, 2 * share), BF16),
            pltpu.VMEM((share, 2 * share), BF16), pltpu.VMEM((share, 2 * share), BF16),
            pltpu.VMEM((OVL, order), BF16), pltpu.VMEM((OVL, order), BF16),
            pltpu.VMEM((6, OVL, OVL), BF16), pltpu.VMEM((6, OVL, OVL), BF16),
            pltpu.SemaphoreType.DMA((6,)),
            pltpu.SemaphoreType.DMA((2 * tiles,)),
            pltpu.SemaphoreType.DMA((copies,)),
            pltpu.SemaphoreType.DMA((copies,)),
        ],
        compiler_params=pltpu.CompilerParams(
            collective_id=0, has_side_effects=True, vmem_limit_bytes=44 * 1024 * 1024
        ),
    )(row_live, column_live, *blocks)
    held = [pltpu.with_memory_space_constraint(a, pltpu.VMEM) for a in held]
    outs = pl.pallas_call(
        put_out,
        out_shape=(win, win, slab, slab, slab, slab),
        in_specs=[vmem] * 2,
        out_specs=(hbm,) * 6,
        scratch_shapes=[pltpu.SemaphoreType.DMA((6,))],
    )(*held)
    return tuple(o[None] for o in outs)


def solution(mesh):
    block = P("diag", "slab", None)

    def shards(*args):
        fits = lax.axis_size("slab") == 4 and lax.axis_size("diag") % 2 == 0
        return (two_chips if fits else many_chips)(*args)

    return jax.shard_map(
        shards, mesh=mesh, in_specs=(block,) * 8 + (P("diag"),) * 2,
        out_specs=(block,) * 6, check_vma=False)
```
